512 devices in a mesh: ctx: 32 (over x_hi, z), fsdp: 16 (over y, x_lo, core).
Axes of the slice: x: 4 (x_hi: 2, x_lo: 2; x = x_hi * 2 + x_lo), y: 4, z: 16, core: 2. Of those that a mesh axis runs over, the one named last changes fastest.
Arguments:
- streams: bfloat16 [3, 16384, 8192], P(None, ('ctx', 'fsdp')), may hold values from -6 to 6
- segments: int32 [16384], replicated, may hold values from 0 to 63, never falling along the last dimension, each value on 1 to 4096 neighbouring positions
- short_taps: float32 [3, 3, 8192], P(None, None, 'fsdp'), may hold values from -3 to 3
- decay_rates: float32 [512, 16], P('fsdp'), may hold values from 1.2207031e-05 to 0.1
- residues: float32 [512, 16], P('fsdp'), may hold values from -2 to 2
- skip_gain: float32 [8192], P('fsdp'), may hold values from -4 to 4
Outputs:
- output: bfloat16 [16384, 8192], P(('ctx', 'fsdp'))
The draws below stay inside these ranges and needn't reach their ends.
Inputs may be any that keep to these rules, and one draw needn't show every extreme that they name: `segments`: never falling along the window; every document has 1 to 4096 tokens and one has exactly 4096.
All inputs are finite; a program needn't handle non-finite values.
Results may differ from the reference program's by a relative error of at most 0.0064.
Values may be sent and summed in bfloat16 or wider, within the bound.
A program may use at most 64 MiB of HBM per device.

```python
import math
import jax
import jax.numpy as jnp
import numpy as np
from jax import lax

D = 8192
GROUP = 16
MODES = 16
SHORT = 3
TOKENS = 16384
DOC_MAX = 4096
DOCS = 64
N_FSDP = 16


def draw_decay_rates(key, part):
    array_shape = (D // GROUP, MODES)
    return jnp.exp(jax.random.uniform(key, array_shape, jnp.float32, jnp.log(0.25 / DOC_MAX), jnp.log(0.1)))


def level_of(key, dims, cuts, least, largest):
    loudness = 1.0
    for position, shards_of in cuts:
        heights = jax.random.uniform(jax.random.fold_in(jax.random.fold_in(key, 6), position), (shards_of,), jnp.float32, least / len(cuts), largest / len(cuts))
        loudness = loudness * jnp.repeat(jnp.exp(heights), dims[position] // shards_of).reshape((-1,) + (1,) * (len(dims) - 1 - position))
    return loudness


def profile(number_of, total, reach, slope):
    portions = [(1 << 20) // math.isqrt(rank ** slope) + 1 for rank in range(2, number_of + 1)]
    surplus, given = total - reach - (number_of - 1), [1] * (number_of - 1)
    while surplus > 0:
        free = [i for i in range(number_of - 1) if given[i] < reach]
        whole, budget = sum([portions[i] for i in free]), surplus
        for i in free:
            more = min(reach - given[i], max(1, budget * portions[i] // whole), surplus)
            given[i] = given[i] + more
            surplus = surplus - more
    return np.array([reach] + given)


def uneven(key, count, total, most, skew):
    if count == 2:
        one = jax.random.randint(key, (), max(1, total - most), min(most, total - 1) + 1)
        return jnp.stack([one, total - one])
    lengths = jnp.asarray(profile(count, total, most, skew), jnp.int32)
    couples = (count - 1) // 2
    donor, taker = lengths[1:1 + 2 * couples:2], lengths[2:2 + 2 * couples:2]
    room = jnp.minimum(donor - 1, most - taker)
    moved = jax.random.randint(jax.random.fold_in(key, 1), (couples,), 0, 1 << 20) % (room + 1)
    lengths = lengths.at[1:1 + 2 * couples:2].set(donor - moved).at[2:2 + 2 * couples:2].set(taker + moved)
    return lengths[jax.random.permutation(jax.random.fold_in(key, 2), count)]


def centred(rng, shape, spread, bound, cuts=(), kind=jnp.bfloat16):
    loudness = level_of(rng, shape, cuts, -0.22, 0.18) if cuts else 1.0
    values = jax.random.normal(rng, shape, jnp.float32) * spread * loudness
    return jnp.minimum(jnp.maximum(values, -bound), bound).astype(kind)


def setup_inputs(seed: int = 0) -> dict:
    key_of = jax.random.split(jax.random.key(seed), 7)
    streams = centred(key_of[0], (3, TOKENS, D), 1.0, 6.0, ((1, 512),))
    segments = jnp.searchsorted(jnp.cumsum(uneven(key_of[1], DOCS, TOKENS, DOC_MAX, 2)), jnp.arange(TOKENS), side="right").astype(jnp.int32)
    short_taps = centred(key_of[2], (3, SHORT, D), 0.6, 3.0, ((2, 16),), jnp.float32)
    decay_rates = draw_decay_rates(jax.random.fold_in(key_of[6], 71), 0)
    residues = centred(key_of[4], (D // GROUP, MODES), 0.35, 2.0, ((0, 16),), jnp.float32)
    skip_gain = centred(key_of[5], (D,), 1.0, 4.0, ((0, 16),), jnp.float32)
    return {"streams": streams, "segments": segments, "short_taps": short_taps, "decay_rates": decay_rates, "residues": residues, "skip_gain": skip_gain}


def featured_stream(stream, stream_taps, earlier_marks):
    values = stream.astype(jnp.float32)
    summed = values * stream_taps[0]
    for offset in range(1, SHORT):
        shifted = jnp.concatenate([jnp.zeros((offset, values.shape[1]), jnp.float32), values[:-offset]], axis=0)
        summed = summed + jnp.where(earlier_marks[offset - 1][:, None], shifted, 0.0) * stream_taps[offset]
    return summed

def reference(streams, segments, short_taps, decay_rates, residues, skip_gain):
    block_width = D // N_FSDP
    block_groups = block_width // GROUP
    earlier_marks = [jnp.concatenate([jnp.full((offset,), -1, jnp.int32), segments[:-offset]]) == segments for offset in range(1, SHORT)]
    continues = earlier_marks[0].astype(jnp.float32)

    def one_block(block_index):
        first_col = block_index * block_width
        columns = lax.dynamic_slice_in_dim(streams, first_col, block_width, 2)
        block_taps = lax.dynamic_slice_in_dim(short_taps, first_col, block_width, 2)
        first_group = block_index * block_groups
        block_rates = lax.dynamic_slice_in_dim(decay_rates, first_group, block_groups, 0)
        block_residues = lax.dynamic_slice_in_dim(residues, first_group, block_groups, 0)
        block_skip = lax.dynamic_slice_in_dim(skip_gain, first_col, block_width, 0)
        queries = featured_stream(columns[0], block_taps[0], earlier_marks).astype(jnp.bfloat16)
        gated_prod = (featured_stream(columns[1], block_taps[1], earlier_marks) * featured_stream(columns[2], block_taps[2], earlier_marks)).astype(jnp.bfloat16)
        queries, gated_prod = lax.optimization_barrier((queries, gated_prod))
        decays = jnp.repeat(jnp.exp(-block_rates), GROUP, axis=0).T
        mode_gain = jnp.repeat(block_residues * jnp.sqrt(-jnp.expm1(-2.0 * block_rates)), GROUP, axis=0).T

        def advance(carried, inputs):
            current, keep_flag = inputs
            carried = keep_flag * decays * carried + current[None, :]
            return (carried, lax.optimization_barrier(jnp.sum(mode_gain * carried, axis=0)))
        start_state = jnp.zeros((MODES, block_width), jnp.float32)
        gated_values = gated_prod.astype(jnp.float32)
        unused, filtered = lax.scan(advance, start_state, (gated_values, continues))
        mixed_out = (filtered + block_skip * gated_values).astype(jnp.bfloat16)
        mixed_out = lax.optimization_barrier(mixed_out)
        return (queries.astype(jnp.float32) * mixed_out.astype(jnp.float32)).astype(jnp.bfloat16)
    blocks = lax.map(one_block, jnp.arange(N_FSDP, dtype=jnp.int32))
    return jnp.transpose(blocks, (1, 0, 2)).reshape(TOKENS, D)
```

```python
import functools

import jax
import jax.numpy as jnp
from jax import lax
from jax.experimental import pallas as pl
from jax.experimental.pallas import tpu as pltpu
from jax.sharding import PartitionSpec as P

MESH = pl.DeviceIdType.MESH
GROUP = 16
MODES = 16
DOC_MAX = 4096
LANES = 128
BLOCK = 128
PACK = LANES // GROUP
F32 = jnp.float32
BF16 = jnp.bfloat16


def iota(shape, dim):
    return lax.broadcasted_iota(jnp.int32, shape, dim)


def halves(value):
    high = value.astype(BF16)
    return high, (value - high.astype(F32)).astype(BF16)


def one_minus_exp_neg(y):
    total = jnp.ones_like(y)
    for order in range(10, 1, -1):
        total = 1.0 - total * y * (1.0 / order)
    return total * y


def fused(
    n_ctx, n_fsdp, rows, look,
    streams, halo, segs, taps, decay, residue, skip, out,
    x, hb, hf, sg, tp, dc, rs, sk, marks, gs, v, qs, ms, mr, inner, fresh, kc, cl, ri, dcy, es, er,
    in_sem, tap_send, tap_recv, halo_send, halo_recv, g_send, g_recv, e_send, e_recv, m_send, m_recv,
):
    ctx, f = lax.axis_index("ctx"), lax.axis_index("fsdp")
    supers, members = n_ctx // 2, 2 * n_fsdp
    tile, half = ctx // 2, lax.rem(ctx, 2)
    r = half * n_fsdp + f
    per = members * rows
    blocks = per // BLOCK
    in_block = BLOCK // rows
    width = v.shape[2]
    lane_tiles = width // LANES
    chunks = x.shape[2] // LANES

    def member(p):
        return (2 * tile + p // n_fsdp, lax.rem(p, n_fsdp))

    def at_super(step):
        return (2 * lax.rem(tile + step, supers) + half, f)

    def tap_copy(owner, to):
        return pltpu.make_async_remote_copy(
            src_ref=tp.at[owner], dst_ref=tp.at[owner], send_sem=tap_send.at[to],
            recv_sem=tap_recv.at[owner], device_id=(ctx, to), device_id_type=MESH,
        )

    first = (r == 0).astype(jnp.int32)
    last = (r == members - 1).astype(jnp.int32)
    after = (
        jnp.where(r == members - 1, 2 * lax.rem(tile + 1, supers), 2 * tile + (r + 1) // n_fsdp),
        lax.rem(f + 1, n_fsdp),
    )

    def halo_copy():
        return pltpu.make_async_remote_copy(
            src_ref=halo, dst_ref=hb, send_sem=halo_send, recv_sem=halo_recv,
            device_id=after, device_id_type=MESH,
        )

    def block_copy(src, dst, sends, recvs, to, slot):
        return pltpu.make_async_remote_copy(
            src_ref=src.at[to], dst_ref=dst.at[slot], send_sem=sends.at[to],
            recv_sem=recvs.at[slot], device_id=member(to), device_id_type=MESH,
        )

    def state_copy(d):
        return pltpu.make_async_remote_copy(
            src_ref=es, dst_ref=er.at[d - 1], send_sem=e_send.at[d - 1],
            recv_sem=e_recv.at[d - 1], device_id=at_super(d), device_id_type=MESH,
        )

    loads = [
        pltpu.make_async_copy(decay, dc, in_sem.at[0]),
        pltpu.make_async_copy(residue, rs, in_sem.at[1]),
        pltpu.make_async_copy(skip, sk, in_sem.at[2]),
        pltpu.make_async_copy(segs, sg, in_sem.at[3]),
        pltpu.make_async_copy(taps, tp.at[f], in_sem.at[4]),
        pltpu.make_async_copy(streams, x, in_sem.at[5]),
    ]
    for load in loads:
        load.start()

    barrier = pltpu.get_barrier_semaphore()

    @pl.loop(1, members)
    def _(k):
        pl.semaphore_signal(
            barrier, inc=1, device_id=member(lax.rem(r + k, members)), device_id_type=MESH
        )

    for d in range(1, look + 1):
        pl.semaphore_signal(barrier, inc=1, device_id=at_super(supers - d), device_id_type=MESH)

    @pl.when(r == 0)
    def _():
        pl.semaphore_signal(
            barrier, inc=1, device_id=(2 * lax.rem(tile + supers - 1, supers) + 1, n_fsdp - 1),
            device_id_type=MESH,
        )

    for load in loads[:4]:
        load.wait()
    square = (BLOCK, BLOCK)
    down, across = iota(square, 0), iota(square, 1)
    eye = down == across
    causal = down >= across
    same_group = (down // MODES) == (across // GROUP)
    away = lax.rem(BLOCK - across, BLOCK).astype(F32)

    def to_column(row):
        return jnp.sum(jnp.where(eye, jnp.broadcast_to(row, square), 0.0), axis=1, keepdims=True)

    def mark_row(index):
        return sg[pl.ds(index, 1), :].astype(F32)

    for m in range(lane_tiles):
        base = half * (lane_tiles * PACK) + m * PACK
        rates = dc[pl.ds(base, PACK), :]
        gains = rs[pl.ds(base, PACK), :] * jnp.sqrt(one_minus_exp_neg(2.0 * rates))

        def spread(small):
            tall = jnp.broadcast_to(small[:, None, :], (PACK, MODES, MODES)).reshape(BLOCK, MODES)
            own = lax.rem(iota((BLOCK, MODES), 0), MODES) == iota((BLOCK, MODES), 1)
            return jnp.sum(jnp.where(own, tall, 0.0), axis=1, keepdims=True)

        rate = jnp.broadcast_to(spread(rates), square)
        gain = jnp.broadcast_to(spread(gains), square)
        rate_row = jnp.sum(jnp.where(eye, rate, 0.0), axis=0, keepdims=True)
        gain_row = jnp.sum(jnp.where(eye, gain, 0.0), axis=0, keepdims=True)
        dcy[m] = rate
        rise = gain_row * jnp.exp(-rate_row * (down + 1).astype(F32))
        high, low = halves(rise)
        ri[m] = jnp.concatenate([high, low, high], axis=1)
        close = jnp.exp(-rate * (BLOCK - 1 - across).astype(F32))
        high, low = halves(close)
        cl[m] = jnp.concatenate([high, low], axis=1)
        taps_of = jnp.sum(
            (gain * jnp.exp(-rate * away)).reshape(PACK, MODES, BLOCK), axis=1
        )
        for g in range(PACK):
            line = jnp.broadcast_to(taps_of[g : g + 1, :], square)
            line = pltpu.roll(line, 0, 1, stride=1, stride_axis=0)
            kc[m, :, g * BLOCK : (g + 1) * BLOCK] = jnp.where(causal, line, 0.0).astype(BF16)

    top = tile * blocks
    before_row = mark_row(jnp.maximum(top - 1, 0))
    before_col = to_column(before_row)[BLOCK - 8 :]
    before_col = jnp.where(tile > 0, before_col, -1.0)
    marks[0:8, :] = jnp.broadcast_to(before_col, (8, LANES))
    for b in range(blocks):
        marks[8 + b * BLOCK : 8 + (b + 1) * BLOCK, :] = jnp.broadcast_to(
            to_column(mark_row(top + b)), square
        )

    loads[4].wait()
    pl.semaphore_wait(barrier, members - 1 + look + last)

    halo_copy().start()

    @pl.loop(1, n_fsdp)
    def _(k):
        tap_copy(f, lax.rem(f + k, n_fsdp)).start()

    loads[5].wait()
    halo_copy().wait_recv()
    hf[...] = hb[...].astype(F32)

    window = marks[pl.ds(pl.multiple_of(r * rows, rows), rows + 8), :]
    own_marks = window[8:]
    agree = [None] + [window[8 - j : 8 - j + rows] == own_marks for j in (1, 2)]
    row_id = iota((rows, LANES), 0)

    def feature(s, owner, lane, chunk):
        col = pl.ds(pl.multiple_of(chunk * LANES, LANES), LANES)
        now = x[s, :, col].astype(F32)
        prev1 = hf[2 * s + 1, pl.ds(chunk, 1), :]
        prev2 = hf[2 * s, pl.ds(chunk, 1), :]
        shift1 = jnp.where(row_id == 0, prev1, pltpu.roll(now, 1, 0))
        shift2 = jnp.where(row_id == 0, prev2, jnp.where(row_id == 1, prev1, pltpu.roll(now, 2, 0)))

        def tap(j):
            return tp[owner, s, pl.ds(j, 1), lane * LANES : (lane + 1) * LANES]

        total = now * tap(0)
        total = total + jnp.where(agree[1], shift1, 0.0) * tap(1)
        return total + jnp.where(agree[2], shift2, 0.0) * tap(2)

    @pl.loop(0, n_fsdp)
    def _(k):
        owner = lax.rem(f + k, n_fsdp)

        @pl.when(k > 0)
        def _():
            tap_copy(owner, f).wait_recv()

        for part in range(2):
            to = part * n_fsdp + owner
            for m in range(lane_tiles):
                lane = part * lane_tiles + m
                chunk = owner * (2 * lane_tiles) + lane
                col = pl.ds(pl.multiple_of(chunk * LANES, LANES), LANES)
                qs[:, col] = feature(0, owner, lane, chunk).astype(BF16)
                gated = feature(1, owner, lane, chunk) * feature(2, owner, lane, chunk)
                gs[to, :, m * LANES : (m + 1) * LANES] = gated.astype(BF16)

            @pl.when(to != r)
            def _():
                block_copy(gs, v, g_send, g_recv, to, r).start()

    v[r] = gs[r]

    def marks_of(b):
        return marks[8 + b * BLOCK : 8 + (b + 1) * BLOCK, :]

    def end_mark(b):
        if b < 0:
            return marks[7:8, :]
        return marks[7 + (b + 1) * BLOCK : 8 + (b + 1) * BLOCK, :]

    def values(b, m):
        four = v[b * in_block : (b + 1) * in_block, :, m * LANES : (m + 1) * LANES]
        return four.reshape(BLOCK, LANES)

    spot = same_group.astype(F32)
    for b in range(blocks):
        for p in range(b * in_block, (b + 1) * in_block):

            @pl.when(r != p)
            def _(p=p):
                block_copy(gs, v, g_send, g_recv, r, p).wait_recv()

        ending = (marks_of(b) == end_mark(b)).astype(F32)
        for m in range(lane_tiles):
            kept = (values(b, m).astype(F32) * ending).astype(BF16)
            fresh[b, m] = spot * jnp.dot(
                cl[m], jnp.concatenate([kept, kept], axis=0), preferred_element_type=F32
            )

    for m in range(lane_tiles):
        fade = jnp.exp(-dcy[m] * float(BLOCK))
        state = fresh[0, m]
        for b in range(1, blocks):
            passing = (end_mark(b) == end_mark(b - 1)).astype(F32)
            state = passing * fade * state + fresh[b, m]
        es[:, m * LANES : (m + 1) * LANES] = jnp.sum(
            state.reshape(PACK, MODES, LANES), axis=0
        )
    for d in range(look, 0, -1):
        state_copy(d).start()

    lane_group = iota((1, LANES), 1) // GROUP
    for b in range(blocks):
        row = jnp.broadcast_to(mark_row(top + b), square)
        agreeing = (marks_of(b) == row).astype(BF16)
        agreeing = jnp.concatenate([agreeing] * PACK, axis=1)
        for m in range(lane_tiles):
            vals = values(b, m)
            parts = [vals * (lane_group == g).astype(BF16) for g in range(PACK)]
            direct = jnp.dot(
                kc[m] * agreeing, jnp.concatenate(parts, axis=0), preferred_element_type=F32
            )
            gain = sk[pl.ds(half * lane_tiles + m, 1), :]
            inner[b, m] = direct + gain * vals.astype(F32)

    first_mark = marks[8:9, :]
    for d in range(1, look + 1):
        state_copy(d).wait_recv()
    states = []
    for m in range(lane_tiles):
        state = jnp.zeros(square, F32)
        for d in range(1, look + 1):
            source = lax.rem(tile + supers - d, supers)
            its_end = mark_row(source * blocks + blocks - 1)[:, LANES - 1 :]
            joined = (jnp.broadcast_to(its_end, (1, LANES)) == first_mark).astype(F32)
            joined = jnp.where(tile >= d, joined, 0.0)
            part = er[d - 1, :, m * LANES : (m + 1) * LANES]
            part = jnp.concatenate([part] * PACK, axis=0)
            if d > 1:
                part = part * jnp.exp(-dcy[m] * float(per * (d - 1)))
            state = state + joined * part
        states.append(spot * state)

    for b in range(blocks):
        follow = (marks_of(b) == end_mark(b - 1)).astype(F32)
        passing = (end_mark(b) == end_mark(b - 1)).astype(F32)
        for m in range(lane_tiles):
            high, low = halves(states[m])
            brought = jnp.dot(
                ri[m], jnp.concatenate([high, high, low], axis=0), preferred_element_type=F32
            )
            mixed = (inner[b, m] + follow * brought).astype(BF16)
            ms[b * in_block : (b + 1) * in_block, :, m * LANES : (m + 1) * LANES] = mixed.reshape(
                in_block, rows, LANES
            )
            if b < blocks - 1:
                fade = jnp.exp(-dcy[m] * float(BLOCK))
                states[m] = passing * fade * states[m] + fresh[b, m]
        for p in range(b * in_block, (b + 1) * in_block):

            @pl.when(r != p)
            def _(p=p):
                block_copy(ms, mr, m_send, m_recv, p, r).start()

    mr[r] = ms[r]

    @pl.loop(0, members)
    def _(k):
        source = lax.rem(r + k, members)

        @pl.when(k > 0)
        def _():
            block_copy(ms, mr, m_send, m_recv, r, source).wait_recv()

        base = lax.rem(source, n_fsdp) * (2 * width) + (source // n_fsdp) * width
        col = pl.ds(pl.multiple_of(base, width), width)
        out[:, col] = (qs[:, col].astype(F32) * mr[source].astype(F32)).astype(BF16)

    halo_copy().wait_send()

    @pl.loop(1, n_fsdp)
    def _(k):
        tap_copy(f, lax.rem(f + k, n_fsdp)).wait_send()

    @pl.loop(1, members)
    def _(k):
        to = lax.rem(r + k, members)
        block_copy(gs, v, g_send, g_recv, to, r).wait_send()
        block_copy(ms, mr, m_send, m_recv, to, r).wait_send()

    for d in range(1, look + 1):
        state_copy(d).wait_send()


def local(streams, segments, short_taps, decay_rates, residues, skip_gain):
    n_ctx, n_fsdp = lax.axis_size("ctx"), lax.axis_size("fsdp")
    rows, model = streams.shape[1:]
    supers, members = n_ctx // 2, 2 * n_fsdp
    width = model // members
    lane_tiles = width // LANES
    per = members * rows
    blocks = per // BLOCK
    look = min(-(-DOC_MAX // per), supers - 1)
    groups = width // GROUP
    halo = streams[:, rows - 2 :, :].reshape(6, model // LANES, LANES)
    segs = segments.reshape(-1, LANES)
    skip = skip_gain.reshape(-1, LANES)
    any_space = pl.BlockSpec(memory_space=pl.ANY)
    dma = pltpu.SemaphoreType.DMA
    square = (BLOCK, BLOCK)
    vmem = pltpu.VMEM
    return pl.pallas_call(
        functools.partial(fused, n_ctx, n_fsdp, rows, look),
        out_shape=jax.ShapeDtypeStruct((rows, model), BF16),
        in_specs=[any_space] * 7,
        out_specs=pl.BlockSpec(memory_space=vmem),
        scratch_shapes=[
            vmem((3, rows, model), BF16),
            vmem((6, model // LANES, LANES), BF16),
            vmem((6, model // LANES, LANES), F32),
            vmem(segs.shape, jnp.int32),
            vmem((n_fsdp, *short_taps.shape), F32),
            vmem(decay_rates.shape, F32),
            vmem(residues.shape, F32),
            vmem(skip.shape, F32),
            vmem((8 + per, LANES), F32),
            vmem((members, rows, width), BF16),
            vmem((members, rows, width), BF16),
            vmem((rows, model), BF16),
            vmem((members, rows, width), BF16),
            vmem((members, rows, width), BF16),
            vmem((blocks, lane_tiles, *square), F32),
            vmem((blocks, lane_tiles, *square), F32),
            vmem((lane_tiles, BLOCK, PACK * BLOCK), BF16),
            vmem((lane_tiles, BLOCK, 2 * BLOCK), BF16),
            vmem((lane_tiles, BLOCK, 3 * BLOCK), BF16),
            vmem((lane_tiles, *square), F32),
            vmem((MODES, width), F32),
            vmem((look, MODES, width), F32),
            dma((6,)),
            dma((n_fsdp,)),
            dma((n_fsdp,)),
            dma(()),
            dma(()),
            dma((members,)),
            dma((members,)),
            dma((look,)),
            dma((look,)),
            dma((members,)),
            dma((members,)),
        ],
        compiler_params=pltpu.CompilerParams(
            collective_id=0, has_side_effects=True, vmem_limit_bytes=48 << 20
        ),
    )(streams, halo, segs, short_taps, decay_rates, residues, skip)


def solution(mesh):
    placed = (
        P(None, ("ctx", "fsdp"), None),
        P(),
        P(None, None, "fsdp"),
        P("fsdp", None),
        P("fsdp", None),
        P("fsdp"),
    )
    return jax.shard_map(
        local, mesh=mesh, in_specs=placed, out_specs=P(("ctx", "fsdp"), None), check_vma=False
    )
```

```python
import functools

import jax
import jax.numpy as jnp
from jax import lax
from jax.experimental import pallas as pl
from jax.experimental.pallas import tpu as pltpu
from jax.sharding import PartitionSpec as P

MESH = pl.DeviceIdType.MESH
GROUP = 16
MODES = 16
DOC_MAX = 4096
LANES = 128
BLOCK = 128
PACK = LANES // GROUP
F32 = jnp.float32
BF16 = jnp.bfloat16


def iota(shape, dim):
    return lax.broadcasted_iota(jnp.int32, shape, dim)


def halves(value):
    high = value.astype(BF16)
    return high, (value - high.astype(F32)).astype(BF16)


def one_minus_exp_neg(y):
    total = jnp.ones_like(y)
    for order in range(10, 1, -1):
        total = 1.0 - total * y * (1.0 / order)
    return total * y


def fused(
    n_ctx, n_fsdp, rows, look,
    streams, segs, taps, decay, residue, skip, out,
    x, hs, hb, hf, sg, own_taps, tp, dc, rs, sk, marks, gs, v, qs, ms, mr, inner, fresh, kc, cl, ri, dcy, carry, es, er,
    in_sem, tap_send, tap_recv, halo_send, halo_recv, g_send, g_recv, e_send, e_recv, m_send, m_recv, hello, ready,
):
    ctx, f = lax.axis_index("ctx"), lax.axis_index("fsdp")
    supers, members = n_ctx // 2, 2 * n_fsdp
    tile, half = ctx // 2, lax.rem(ctx, 2)
    r = half * n_fsdp + f
    per = members * rows
    blocks = per // BLOCK
    in_block = BLOCK // rows
    width = v.shape[2]
    lane_tiles = width // LANES
    quads = own_taps.shape[2] // LANES

    def member(p):
        return (2 * tile + p // n_fsdp, lax.rem(p, n_fsdp))

    def at_super(step):
        return (ctx + 2 * step, f)

    def tap_copy(owner, to):
        return pltpu.make_async_remote_copy(
            src_ref=tp.at[owner], dst_ref=tp.at[owner], send_sem=tap_send.at[to],
            recv_sem=tap_recv.at[owner], device_id=(ctx, to), device_id_type=MESH,
        )

    more = tile < supers - 1
    sends_halo = more | (r < members - 1)
    gets_halo = (tile > 0) | (r > 0)

    def halo_copy():
        return pltpu.make_async_remote_copy(
            src_ref=hs, dst_ref=hb, send_sem=halo_send, recv_sem=halo_recv,
            device_id=(2 * tile + (r + 1) // n_fsdp, lax.rem(f + 1, n_fsdp)), device_id_type=MESH,
        )

    def block_copy(src, dst, sends, recvs, to, slot):
        return pltpu.make_async_remote_copy(
            src_ref=src.at[to], dst_ref=dst.at[slot], send_sem=sends.at[to],
            recv_sem=recvs.at[slot], device_id=member(to), device_id_type=MESH,
        )

    def pass_ready(hop):
        if hop > look:
            return
        known = tile + hop < supers
        if hop == 1:

            @pl.when(tile > 0)
            def _():
                pl.semaphore_wait(hello, 1)

        else:

            @pl.when(known)
            def _():
                pl.semaphore_wait(ready.at[hop - 2], 1)

        if hop < look:

            @pl.when(known & (tile > 0))
            def _():
                pl.semaphore_signal(
                    ready.at[hop - 1], inc=1, device_id=at_super(-1), device_id_type=MESH
                )

    def state_copy(d):
        return pltpu.make_async_remote_copy(
            src_ref=es, dst_ref=er.at[d - 1], send_sem=e_send.at[d - 1],
            recv_sem=e_recv.at[d - 1], device_id=at_super(d), device_id_type=MESH,
        )

    loads = [
        pltpu.make_async_copy(decay, dc, in_sem.at[0]),
        pltpu.make_async_copy(residue, rs, in_sem.at[1]),
        pltpu.make_async_copy(skip, sk, in_sem.at[2]),
        pltpu.make_async_copy(segs, sg, in_sem.at[3]),
        pltpu.make_async_copy(taps, own_taps, in_sem.at[4]),
        pltpu.make_async_copy(streams, x, in_sem.at[5]),
    ]
    for load in loads:
        load.start()

    barrier = pltpu.get_barrier_semaphore()

    @pl.loop(1, members)
    def _(k):
        pl.semaphore_signal(
            barrier, inc=1, device_id=member(lax.rem(r + k, members)), device_id_type=MESH
        )

    @pl.when(tile > 0)
    def _():
        pl.semaphore_signal(barrier, inc=1, device_id=at_super(-1), device_id_type=MESH)

    @pl.when((tile > 0) & (r == 0))
    def _():
        pl.semaphore_signal(
            barrier, inc=1, device_id=(2 * tile - 1, n_fsdp - 1), device_id_type=MESH
        )

    for load in loads[:4]:
        load.wait()
    square = (BLOCK, BLOCK)
    down, across = iota(square, 0), iota(square, 1)
    eye = down == across
    causal = down >= across
    same_group = (down // MODES) == (across // GROUP)
    away = lax.rem(BLOCK - across, BLOCK).astype(F32)

    def to_column(row):
        return jnp.sum(jnp.where(eye, jnp.broadcast_to(row, square), 0.0), axis=1, keepdims=True)

    def mark_row(index):
        return sg[pl.ds(index, 1), :].astype(F32)

    rates = dc[...]
    gains = rs[...] * jnp.sqrt(one_minus_exp_neg(2.0 * rates))
    for m in range(lane_tiles):
        base = half * (lane_tiles * PACK) + m * PACK
        own = iota((BLOCK, rates.shape[1]), 1) == base + iota((BLOCK, rates.shape[1]), 0) // MODES

        def spread(small):
            tall = jnp.concatenate([small] * PACK, axis=0)
            return jnp.sum(jnp.where(own, tall, 0.0), axis=1, keepdims=True)

        rate = jnp.broadcast_to(spread(rates), square)
        gain = jnp.broadcast_to(spread(gains), square)
        rate_row = jnp.sum(jnp.where(eye, rate, 0.0), axis=0, keepdims=True)
        gain_row = jnp.sum(jnp.where(eye, gain, 0.0), axis=0, keepdims=True)
        dcy[m] = rate
        rise = gain_row * jnp.exp(-rate_row * (down + 1).astype(F32))
        high, low = halves(rise)
        ri[m] = jnp.concatenate([high, low, high], axis=1)
        close = jnp.exp(-rate * (BLOCK - 1 - across).astype(F32))
        high, low = halves(close)
        cl[m] = jnp.concatenate([high, low], axis=1)
        taps_of = jnp.sum(
            (gain * jnp.exp(-rate * away)).reshape(PACK, MODES, BLOCK), axis=1
        )
        for g in range(PACK):
            line = jnp.broadcast_to(taps_of[g : g + 1, :], square)
            line = pltpu.roll(line, 0, 1, stride=1, stride_axis=0)
            kc[m, :, g * BLOCK : (g + 1) * BLOCK] = jnp.where(causal, line, 0.0).astype(BF16)

    top = tile * blocks
    before_row = mark_row(jnp.maximum(top - 1, 0))
    before_col = to_column(before_row)[BLOCK - 8 :]
    before_col = jnp.where(tile > 0, before_col, -1.0)
    marks[0:8, :] = jnp.broadcast_to(before_col, (8, LANES))
    for b in range(blocks):
        marks[8 + b * BLOCK : 8 + (b + 1) * BLOCK, :] = jnp.broadcast_to(
            to_column(mark_row(top + b)), square
        )

    loads[4].wait()
    for s in range(3):
        for j in range(3):
            for q in range(quads):
                row = (s * 3 + j) * quads + q
                tp[f, row : row + 1, :] = own_taps[s, j : j + 1, q * LANES : (q + 1) * LANES]

    loads[5].wait()
    step = 4 * LANES
    slot = iota((8, step), 0) // 2

    @pl.loop(0, x.shape[2] // step)
    def _(k):
        col = pl.ds(pl.multiple_of(k * step, step), step)
        total = jnp.zeros((8, step), F32)
        for s in range(3):
            tail = x[s, rows - 8 : rows, col].astype(F32)
            total = jnp.where(slot == s, pltpu.roll(tail, 2 * s + 2, 0), total)
        hs[:, col] = total.astype(BF16)

    greets = jnp.where(more, 1, 0) + jnp.where(more & (r == members - 1), 1, 0)
    pl.semaphore_wait(barrier, members - 1 + greets)

    @pl.when(sends_halo)
    def _():
        halo_copy().start()

    @pl.loop(1, n_fsdp)
    def _(k):
        tap_copy(f, lax.rem(f + k, n_fsdp)).start()

    @pl.when(more)
    def _():
        pl.semaphore_signal(hello, inc=1, device_id=at_super(1), device_id_type=MESH)

    @pl.when(gets_halo)
    def _():
        halo_copy().wait_recv()
        hf[...] = hb[...].astype(F32)

    @pl.when(jnp.logical_not(gets_halo))
    def _():
        hf[...] = jnp.zeros_like(hf)

    pass_ready(1)

    window = marks[pl.ds(pl.multiple_of(r * rows, rows), rows + 8), :]
    own_marks = window[8:]
    agree = [None] + [window[8 - j : 8 - j + rows] == own_marks for j in (1, 2)]
    row_id = iota((rows, LANES), 0)

    def feature(s, owner, lane, chunk):
        col = pl.ds(pl.multiple_of(chunk * LANES, LANES), LANES)
        now = x[s, :, col].astype(F32)
        prev1 = hf[2 * s + 1 : 2 * s + 2, col]
        prev2 = hf[2 * s : 2 * s + 1, col]
        shift1 = jnp.where(row_id == 0, prev1, pltpu.roll(now, 1, 0))
        shift2 = jnp.where(row_id == 0, prev2, jnp.where(row_id == 1, prev1, pltpu.roll(now, 2, 0)))

        def tap(j):
            row = (s * 3 + j) * quads + lane
            return tp[owner, row : row + 1, :]

        total = now * tap(0)
        total = total + jnp.where(agree[1], shift1, 0.0) * tap(1)
        return total + jnp.where(agree[2], shift2, 0.0) * tap(2)

    @pl.loop(0, n_fsdp)
    def _(k):
        owner = lax.rem(f + k, n_fsdp)

        @pl.when(k > 0)
        def _():
            tap_copy(owner, f).wait_recv()

        for part in range(2):
            to = part * n_fsdp + owner
            for m in range(lane_tiles):
                lane = part * lane_tiles + m
                chunk = owner * (2 * lane_tiles) + lane
                col = pl.ds(pl.multiple_of(chunk * LANES, LANES), LANES)
                qs[:, col] = feature(0, owner, lane, chunk).astype(BF16)
                gated = feature(1, owner, lane, chunk) * feature(2, owner, lane, chunk)
                gs[to, :, m * LANES : (m + 1) * LANES] = gated.astype(BF16)

            @pl.when(to != r)
            def _():
                block_copy(gs, v, g_send, g_recv, to, r).start()

    pass_ready(2)
    v[r] = gs[r]

    def marks_of(b):
        return marks[8 + b * BLOCK : 8 + (b + 1) * BLOCK, :]

    def end_mark(b):
        if b < 0:
            return marks[7:8, :]
        return marks[7 + (b + 1) * BLOCK : 8 + (b + 1) * BLOCK, :]

    def values(b, m):
        four = v[b * in_block : (b + 1) * in_block, :, m * LANES : (m + 1) * LANES]
        return four.reshape(BLOCK, LANES)

    spot = same_group.astype(F32)
    for b in range(blocks):
        for p in range(b * in_block, (b + 1) * in_block):

            @pl.when(r != p)
            def _(p=p):
                block_copy(gs, v, g_send, g_recv, r, p).wait_recv()

        ending = (marks_of(b) == end_mark(b)).astype(F32)
        for m in range(lane_tiles):
            kept = (values(b, m).astype(F32) * ending).astype(BF16)
            fresh[b, m] = spot * jnp.dot(
                cl[m], jnp.concatenate([kept, kept], axis=0), preferred_element_type=F32
            )

    pass_ready(3)
    for m in range(lane_tiles):
        fade = jnp.exp(-dcy[m] * float(BLOCK))
        state = fresh[0, m]
        for b in range(1, blocks):
            passing = (end_mark(b) == end_mark(b - 1)).astype(F32)
            state = passing * fade * state + fresh[b, m]
        es[:, m * LANES : (m + 1) * LANES] = jnp.sum(
            state.reshape(PACK, MODES, LANES), axis=0
        )
    for hop in range(4, look + 1):
        pass_ready(hop)
    for d in range(look, 0, -1):

        @pl.when(tile + d < supers)
        def _(d=d):
            state_copy(d).start()


    lane_group = iota((1, LANES), 1) // GROUP
    for b in range(blocks):
        row = jnp.broadcast_to(mark_row(top + b), square)
        agreeing = (marks_of(b) == row).astype(BF16)
        agreeing = jnp.concatenate([agreeing] * PACK, axis=1)
        for m in range(lane_tiles):
            vals = values(b, m)
            parts = [vals * (lane_group == g).astype(BF16) for g in range(PACK)]
            direct = jnp.dot(
                kc[m] * agreeing, jnp.concatenate(parts, axis=0), preferred_element_type=F32
            )
            gain = sk[pl.ds(half * lane_tiles + m, 1), :]
            inner[b, m] = direct + gain * vals.astype(F32)

    first_mark = marks[8:9, :]
    for m in range(lane_tiles):
        carry[m] = jnp.zeros(square, F32)
    for d in range(1, look + 1):

        @pl.when(tile >= d)
        def _(d=d):
            state_copy(d).wait_recv()
            its_end = mark_row((tile - d) * blocks + blocks - 1)[:, LANES - 1 :]
            joined = spot * (jnp.broadcast_to(its_end, (1, LANES)) == first_mark).astype(F32)
            for m in range(lane_tiles):
                part = er[d - 1, :, m * LANES : (m + 1) * LANES]
                part = joined * jnp.concatenate([part] * PACK, axis=0)
                if d > 1:
                    part = part * jnp.exp(-dcy[m] * float(per * (d - 1)))
                carry[m] += part

    states = [carry[m] for m in range(lane_tiles)]

    for b in range(blocks):
        follow = (marks_of(b) == end_mark(b - 1)).astype(F32)
        passing = (end_mark(b) == end_mark(b - 1)).astype(F32)
        for m in range(lane_tiles):
            high, low = halves(states[m])
            brought = jnp.dot(
                ri[m], jnp.concatenate([high, high, low], axis=0), preferred_element_type=F32
            )
            mixed = (inner[b, m] + follow * brought).astype(BF16)
            ms[b * in_block : (b + 1) * in_block, :, m * LANES : (m + 1) * LANES] = mixed.reshape(
                in_block, rows, LANES
            )
            if b < blocks - 1:
                fade = jnp.exp(-dcy[m] * float(BLOCK))
                states[m] = passing * fade * states[m] + fresh[b, m]
        for p in range(b * in_block, (b + 1) * in_block):

            @pl.when(r != p)
            def _(p=p):
                block_copy(ms, mr, m_send, m_recv, p, r).start()

    mr[r] = ms[r]

    @pl.loop(0, members)
    def _(k):
        source = lax.rem(r + k, members)

        @pl.when(k > 0)
        def _():
            block_copy(ms, mr, m_send, m_recv, r, source).wait_recv()

        base = lax.rem(source, n_fsdp) * (2 * width) + (source // n_fsdp) * width
        col = pl.ds(pl.multiple_of(base, width), width)
        out[:, col] = (qs[:, col].astype(F32) * mr[source].astype(F32)).astype(BF16)

    @pl.when(sends_halo)
    def _():
        halo_copy().wait_send()

    @pl.loop(1, n_fsdp)
    def _(k):
        tap_copy(f, lax.rem(f + k, n_fsdp)).wait_send()

    @pl.loop(1, members)
    def _(k):
        to = lax.rem(r + k, members)
        block_copy(gs, v, g_send, g_recv, to, r).wait_send()
        block_copy(ms, mr, m_send, m_recv, to, r).wait_send()

    for d in range(1, look + 1):

        @pl.when(tile + d < supers)
        def _(d=d):
            state_copy(d).wait_send()


def local(streams, segments, short_taps, decay_rates, residues, skip_gain):
    n_ctx, n_fsdp = lax.axis_size("ctx"), lax.axis_size("fsdp")
    rows, model = streams.shape[1:]
    supers, members = n_ctx // 2, 2 * n_fsdp
    width = model // members
    lane_tiles = width // LANES
    per = members * rows
    blocks = per // BLOCK
    look = min(-(-DOC_MAX // per), supers - 1)
    groups = width // GROUP
    segs = segments.reshape(-1, LANES)
    skip = skip_gain.reshape(-1, LANES)
    rates, gains = decay_rates.T, residues.T
    any_space = pl.BlockSpec(memory_space=pl.ANY)
    dma = pltpu.SemaphoreType.DMA
    square = (BLOCK, BLOCK)
    vmem = pltpu.VMEM
    return pl.pallas_call(
        functools.partial(fused, n_ctx, n_fsdp, rows, look),
        out_shape=jax.ShapeDtypeStruct((rows, model), BF16),
        in_specs=[any_space] * 6,
        out_specs=pl.BlockSpec(memory_space=vmem),
        scratch_shapes=[
            vmem((3, rows, model), BF16),
            vmem((8, model), BF16),
            vmem((8, model), BF16),
            vmem((8, model), F32),
            vmem(segs.shape, jnp.int32),
            vmem(short_taps.shape, F32),
            vmem((n_fsdp, -(-9 * (short_taps.shape[2] // LANES) // 8) * 8, LANES), F32),
            vmem(rates.shape, F32),
            vmem(rates.shape, F32),
            vmem(skip.shape, F32),
            vmem((8 + per, LANES), F32),
            vmem((members, rows, width), BF16),
            vmem((members, rows, width), BF16),
            vmem((rows, model), BF16),
            vmem((members, rows, width), BF16),
            vmem((members, rows, width), BF16),
            vmem((blocks, lane_tiles, *square), F32),
            vmem((blocks, lane_tiles, *square), F32),
            vmem((lane_tiles, BLOCK, PACK * BLOCK), BF16),
            vmem((lane_tiles, BLOCK, 2 * BLOCK), BF16),
            vmem((lane_tiles, BLOCK, 3 * BLOCK), BF16),
            vmem((lane_tiles, *square), F32),
            vmem((lane_tiles, *square), F32),
            vmem((MODES, width), F32),
            vmem((look, MODES, width), F32),
            dma((6,)),
            dma((n_fsdp,)),
            dma((n_fsdp,)),
            dma(()),
            dma(()),
            dma((members,)),
            dma((members,)),
            dma((look,)),
            dma((look,)),
            dma((members,)),
            dma((members,)),
            pltpu.SemaphoreType.REGULAR,
            pltpu.SemaphoreType.REGULAR((max(look - 1, 1),)),
        ],
        compiler_params=pltpu.CompilerParams(
            collective_id=0, has_side_effects=True, vmem_limit_bytes=60 * 1024 * 1024
        ),
    )(streams, segs, short_taps, rates, gains, skip)


def solution(mesh):
    placed = (
        P(None, ("ctx", "fsdp"), None),
        P(),
        P(None, None, "fsdp"),
        P("fsdp", None),
        P("fsdp", None),
        P("fsdp"),
    )
    return jax.shard_map(
        local, mesh=mesh, in_specs=placed, out_specs=P(("ctx", "fsdp"), None), check_vma=False
    )
```

```python
import functools

import jax
import jax.numpy as jnp
from jax import lax
from jax.experimental import pallas as pl
from jax.experimental.pallas import tpu as pltpu
from jax.sharding import PartitionSpec as P

MESH = pl.DeviceIdType.MESH
GROUP = 16
MODES = 16
DOC_MAX = 4096
LANES = 128
BLOCK = 128
PACK = LANES // GROUP
F32 = jnp.float32
BF16 = jnp.bfloat16


def iota(shape, dim):
    return lax.broadcasted_iota(jnp.int32, shape, dim)


def halves(value):
    high = value.astype(BF16)
    return high, (value - high.astype(F32)).astype(BF16)


def one_minus_exp_neg(y):
    total = jnp.ones_like(y)
    for order in range(10, 1, -1):
        total = 1.0 - total * y * (1.0 / order)
    return total * y


def fused(
    n_ctx, n_fsdp, rows, look,
    streams, segs, taps, decay, residue, skip, out,
    x, hs, hb, hf, sg, own_taps, tp, dc, rs, sk, marks, gs, v, qs, ms, mr, inner, fresh, kc, cl, ri, dcy, carry, es, er,
    in_sem, tap_send, tap_recv, halo_send, halo_recv, g_send, g_recv, e_send, e_recv, m_send, m_recv, hello, ready,
):
    ctx, f = lax.axis_index("ctx"), lax.axis_index("fsdp")
    supers, members = n_ctx // 2, 2 * n_fsdp
    tile, half = ctx // 2, lax.rem(ctx, 2)
    r = half * n_fsdp + f
    per = members * rows
    blocks = per // BLOCK
    in_block = BLOCK // rows
    width = v.shape[2]
    lane_tiles = width // LANES
    quads = own_taps.shape[2] // LANES

    def member(p):
        return (2 * tile + p // n_fsdp, lax.rem(p, n_fsdp))

    def at_super(step):
        return (ctx + 2 * step, f)

    def tap_copy(owner, to):
        return pltpu.make_async_remote_copy(
            src_ref=tp.at[owner], dst_ref=tp.at[owner], send_sem=tap_send.at[to],
            recv_sem=tap_recv.at[owner], device_id=(ctx, to), device_id_type=MESH,
        )

    more = tile < supers - 1
    sends_halo = more | (r < members - 1)
    gets_halo = (tile > 0) | (r > 0)

    def halo_copy():
        return pltpu.make_async_remote_copy(
            src_ref=hs, dst_ref=hb, send_sem=halo_send, recv_sem=halo_recv,
            device_id=(2 * tile + (r + 1) // n_fsdp, lax.rem(f + 1, n_fsdp)), device_id_type=MESH,
        )

    def block_copy(src, dst, sends, recvs, to, slot):
        return pltpu.make_async_remote_copy(
            src_ref=src.at[to], dst_ref=dst.at[slot], send_sem=sends.at[to],
            recv_sem=recvs.at[slot], device_id=member(to), device_id_type=MESH,
        )

    def pass_ready(hop):
        if hop > look:
            return
        known = tile + hop < supers
        if hop == 1:

            @pl.when(tile > 0)
            def _():
                pl.semaphore_wait(hello, 1)

        else:

            @pl.when(known)
            def _():
                pl.semaphore_wait(ready.at[hop - 2], 1)

        if hop < look:

            @pl.when(known & (tile > 0))
            def _():
                pl.semaphore_signal(
                    ready.at[hop - 1], inc=1, device_id=at_super(-1), device_id_type=MESH
                )

    def state_copy(d):
        return pltpu.make_async_remote_copy(
            src_ref=es, dst_ref=er.at[d - 1], send_sem=e_send.at[d - 1],
            recv_sem=e_recv.at[d - 1], device_id=at_super(d), device_id_type=MESH,
        )

    loads = [
        pltpu.make_async_copy(decay, dc, in_sem.at[0]),
        pltpu.make_async_copy(residue, rs, in_sem.at[1]),
        pltpu.make_async_copy(skip, sk, in_sem.at[2]),
        pltpu.make_async_copy(segs, sg, in_sem.at[3]),
        pltpu.make_async_copy(taps, own_taps, in_sem.at[4]),
        pltpu.make_async_copy(streams, x, in_sem.at[5]),
    ]
    for load in loads:
        load.start()

    barrier = pltpu.get_barrier_semaphore()

    @pl.loop(1, members)
    def _(k):
        pl.semaphore_signal(
            barrier, inc=1, device_id=member(lax.rem(r + k, members)), device_id_type=MESH
        )

    @pl.when(tile > 0)
    def _():
        pl.semaphore_signal(barrier, inc=1, device_id=at_super(-1), device_id_type=MESH)

    @pl.when((tile > 0) & (r == 0))
    def _():
        pl.semaphore_signal(
            barrier, inc=1, device_id=(2 * tile - 1, n_fsdp - 1), device_id_type=MESH
        )

    loads[4].wait()
    for s in range(3):
        for j in range(3):
            for q in range(quads):
                row = (s * 3 + j) * quads + q
                tp[f, row : row + 1, :] = own_taps[s, j : j + 1, q * LANES : (q + 1) * LANES]

    greets = jnp.where(more, 1, 0) + jnp.where(more & (r == members - 1), 1, 0)
    pl.semaphore_wait(barrier, members - 1 + greets)

    @pl.loop(1, n_fsdp)
    def _(k):
        tap_copy(f, lax.rem(f + k, n_fsdp)).start()

    loads[5].wait()
    step = 4 * LANES
    slot = iota((8, step), 0) // 2

    @pl.loop(0, x.shape[2] // step)
    def _(k):
        col = pl.ds(pl.multiple_of(k * step, step), step)
        total = jnp.zeros((8, step), F32)
        for s in range(3):
            tail = x[s, rows - 8 : rows, col].astype(F32)
            total = jnp.where(slot == s, pltpu.roll(tail, 2 * s + 2, 0), total)
        hs[:, col] = total.astype(BF16)

    @pl.when(sends_halo)
    def _():
        halo_copy().start()

    @pl.when(more)
    def _():
        pl.semaphore_signal(hello, inc=1, device_id=at_super(1), device_id_type=MESH)

    for load in loads[:4]:
        load.wait()
    square = (BLOCK, BLOCK)
    down, across = iota(square, 0), iota(square, 1)
    eye = down == across
    causal = down >= across
    same_group = (down // MODES) == (across // GROUP)
    away = lax.rem(BLOCK - across, BLOCK).astype(F32)

    def to_column(row):
        return jnp.sum(jnp.where(eye, jnp.broadcast_to(row, square), 0.0), axis=1, keepdims=True)

    def mark_row(index):
        return sg[pl.ds(index, 1), :].astype(F32)

    rates = dc[...]
    gains = rs[...] * jnp.sqrt(one_minus_exp_neg(2.0 * rates))
    for m in range(lane_tiles):
        base = half * (lane_tiles * PACK) + m * PACK
        own = iota((BLOCK, rates.shape[1]), 1) == base + iota((BLOCK, rates.shape[1]), 0) // MODES

        def spread(small):
            tall = jnp.concatenate([small] * PACK, axis=0)
            return jnp.sum(jnp.where(own, tall, 0.0), axis=1, keepdims=True)

        rate = jnp.broadcast_to(spread(rates), square)
        gain = jnp.broadcast_to(spread(gains), square)
        rate_row = jnp.sum(jnp.where(eye, rate, 0.0), axis=0, keepdims=True)
        gain_row = jnp.sum(jnp.where(eye, gain, 0.0), axis=0, keepdims=True)
        dcy[m] = rate
        rise = gain_row * jnp.exp(-rate_row * (down + 1).astype(F32))
        high, low = halves(rise)
        ri[m] = jnp.concatenate([high, low, high], axis=1)
        close = jnp.exp(-rate * (BLOCK - 1 - across).astype(F32))
        high, low = halves(close)
        cl[m] = jnp.concatenate([high, low], axis=1)
        taps_of = jnp.sum(
            (gain * jnp.exp(-rate * away)).reshape(PACK, MODES, BLOCK), axis=1
        )
        for g in range(PACK):
            line = jnp.broadcast_to(taps_of[g : g + 1, :], square)
            line = pltpu.roll(line, 0, 1, stride=1, stride_axis=0)
            kc[m, :, g * BLOCK : (g + 1) * BLOCK] = jnp.where(causal, line, 0.0).astype(BF16)

    top = tile * blocks
    before_row = mark_row(jnp.maximum(top - 1, 0))
    before_col = to_column(before_row)[BLOCK - 8 :]
    before_col = jnp.where(tile > 0, before_col, -1.0)
    marks[0:8, :] = jnp.broadcast_to(before_col, (8, LANES))
    for b in range(blocks):
        marks[8 + b * BLOCK : 8 + (b + 1) * BLOCK, :] = jnp.broadcast_to(
            to_column(mark_row(top + b)), square
        )

    @pl.when(gets_halo)
    def _():
        halo_copy().wait_recv()
        hf[...] = hb[...].astype(F32)

    @pl.when(jnp.logical_not(gets_halo))
    def _():
        hf[...] = jnp.zeros_like(hf)

    pass_ready(1)

    window = marks[pl.ds(pl.multiple_of(r * rows, rows), rows + 8), :]
    own_marks = window[8:]
    agree = [None] + [window[8 - j : 8 - j + rows] == own_marks for j in (1, 2)]
    row_id = iota((rows, LANES), 0)

    def feature(s, owner, lane, chunk):
        col = pl.ds(pl.multiple_of(chunk * LANES, LANES), LANES)
        now = x[s, :, col].astype(F32)
        prev1 = hf[2 * s + 1 : 2 * s + 2, col]
        prev2 = hf[2 * s : 2 * s + 1, col]
        shift1 = jnp.where(row_id == 0, prev1, pltpu.roll(now, 1, 0))
        shift2 = jnp.where(row_id == 0, prev2, jnp.where(row_id == 1, prev1, pltpu.roll(now, 2, 0)))

        def tap(j):
            row = (s * 3 + j) * quads + lane
            return tp[owner, row : row + 1, :]

        total = now * tap(0)
        total = total + jnp.where(agree[1], shift1, 0.0) * tap(1)
        return total + jnp.where(agree[2], shift2, 0.0) * tap(2)

    @pl.loop(0, n_fsdp)
    def _(k):
        owner = lax.rem(f + n_fsdp - k, n_fsdp)

        @pl.when(k > 0)
        def _():
            tap_copy(owner, f).wait_recv()

        for hop, point in ((2, n_fsdp // 4), (3, n_fsdp // 2)):

            @pl.when(k == point)
            def _(hop=hop):
                pass_ready(hop)

        for part in range(2):
            to = part * n_fsdp + owner
            for m in range(lane_tiles):
                lane = part * lane_tiles + m
                chunk = owner * (2 * lane_tiles) + lane
                col = pl.ds(pl.multiple_of(chunk * LANES, LANES), LANES)
                qs[:, col] = feature(0, owner, lane, chunk).astype(BF16)
                gated = feature(1, owner, lane, chunk) * feature(2, owner, lane, chunk)
                gs[to, :, m * LANES : (m + 1) * LANES] = gated.astype(BF16)

            @pl.when(to != r)
            def _():
                block_copy(gs, v, g_send, g_recv, to, r).start()

    v[r] = gs[r]

    def marks_of(b):
        return marks[8 + b * BLOCK : 8 + (b + 1) * BLOCK, :]

    def end_mark(b):
        if b < 0:
            return marks[7:8, :]
        return marks[7 + (b + 1) * BLOCK : 8 + (b + 1) * BLOCK, :]

    def values(b, m):
        four = v[b * in_block : (b + 1) * in_block, :, m * LANES : (m + 1) * LANES]
        return four.reshape(BLOCK, LANES)

    spot = same_group.astype(F32)
    for b in range(blocks):
        for p in range(b * in_block, (b + 1) * in_block):

            @pl.when(r != p)
            def _(p=p):
                block_copy(gs, v, g_send, g_recv, r, p).wait_recv()

        ending = (marks_of(b) == end_mark(b)).astype(F32)
        for m in range(lane_tiles):
            kept = (values(b, m).astype(F32) * ending).astype(BF16)
            fresh[b, m] = spot * jnp.dot(
                cl[m], jnp.concatenate([kept, kept], axis=0), preferred_element_type=F32
            )

    for m in range(lane_tiles):
        fade = jnp.exp(-dcy[m] * float(BLOCK))
        state = fresh[0, m]
        for b in range(1, blocks):
            passing = (end_mark(b) == end_mark(b - 1)).astype(F32)
            state = passing * fade * state + fresh[b, m]
        es[:, m * LANES : (m + 1) * LANES] = jnp.sum(
            state.reshape(PACK, MODES, LANES), axis=0
        ).astype(BF16)
    for hop in range(4, look + 1):
        pass_ready(hop)
    for d in range(1, look + 1):

        @pl.when(tile + d < supers)
        def _(d=d):
            state_copy(d).start()


    lane_group = iota((1, LANES), 1) // GROUP
    for b in range(blocks):
        row = jnp.broadcast_to(mark_row(top + b), square)
        agreeing = (marks_of(b) == row).astype(BF16)
        agreeing = jnp.concatenate([agreeing] * PACK, axis=1)
        for m in range(lane_tiles):
            vals = values(b, m)
            parts = [vals * (lane_group == g).astype(BF16) for g in range(PACK)]
            direct = jnp.dot(
                kc[m] * agreeing, jnp.concatenate(parts, axis=0), preferred_element_type=F32
            )
            gain = sk[pl.ds(half * lane_tiles + m, 1), :]
            inner[b, m] = direct + gain * vals.astype(F32)

    first_mark = marks[8:9, :]
    for m in range(lane_tiles):
        carry[m] = jnp.zeros(square, F32)
    for d in range(1, look + 1):

        @pl.when(tile >= d)
        def _(d=d):
            state_copy(d).wait_recv()
            its_end = mark_row((tile - d) * blocks + blocks - 1)[:, LANES - 1 :]
            joined = spot * (jnp.broadcast_to(its_end, (1, LANES)) == first_mark).astype(F32)
            for m in range(lane_tiles):
                part = er[d - 1, :, m * LANES : (m + 1) * LANES].astype(F32)
                part = joined * jnp.concatenate([part] * PACK, axis=0)
                if d > 1:
                    part = part * jnp.exp(-dcy[m] * float(per * (d - 1)))
                carry[m] += part

    for m in range(lane_tiles):
        state = carry[m]
        fade = jnp.exp(-dcy[m] * float(BLOCK))
        for b in range(blocks):
            kept = fresh[b, m]
            fresh[b, m] = state
            if b < blocks - 1:
                passing = (end_mark(b) == end_mark(b - 1)).astype(F32)
                state = passing * fade * state + kept

    @pl.loop(0, blocks)
    def _(k):
        b = lax.rem(r // in_block + k, blocks)
        start = pl.multiple_of(b * BLOCK, BLOCK)
        follow = (marks[pl.ds(start + 8, BLOCK), :] == marks[pl.ds(start, 8), :][7:]).astype(F32)
        for m in range(lane_tiles):
            high, low = halves(fresh[b, m])
            brought = jnp.dot(
                ri[m], jnp.concatenate([high, high, low], axis=0), preferred_element_type=F32
            )
            mixed = (inner[b, m] + follow * brought).astype(BF16)
            ms[pl.ds(b * in_block, in_block), :, m * LANES : (m + 1) * LANES] = mixed.reshape(
                in_block, rows, LANES
            )
        for q in range(in_block):
            to = b * in_block + q

            @pl.when(r != to)
            def _(to=to):
                block_copy(ms, mr, m_send, m_recv, to, r).start()

    mr[r] = ms[r]

    @pl.loop(0, members)
    def _(k):
        source = lax.rem(r + members - k, members)

        @pl.when(k > 0)
        def _():
            block_copy(ms, mr, m_send, m_recv, r, source).wait_recv()

        base = lax.rem(source, n_fsdp) * (2 * width) + (source // n_fsdp) * width
        col = pl.ds(pl.multiple_of(base, width), width)
        out[:, col] = (qs[:, col].astype(F32) * mr[source].astype(F32)).astype(BF16)

    @pl.when(sends_halo)
    def _():
        halo_copy().wait_send()

    @pl.loop(1, n_fsdp)
    def _(k):
        tap_copy(f, lax.rem(f + k, n_fsdp)).wait_send()

    @pl.loop(1, members)
    def _(k):
        to = lax.rem(r + k, members)
        block_copy(gs, v, g_send, g_recv, to, r).wait_send()
        block_copy(ms, mr, m_send, m_recv, to, r).wait_send()

    for d in range(1, look + 1):

        @pl.when(tile + d < supers)
        def _(d=d):
            state_copy(d).wait_send()


def local(streams, segments, short_taps, decay_rates, residues, skip_gain):
    n_ctx, n_fsdp = lax.axis_size("ctx"), lax.axis_size("fsdp")
    rows, model = streams.shape[1:]
    supers, members = n_ctx // 2, 2 * n_fsdp
    width = model // members
    lane_tiles = width // LANES
    per = members * rows
    blocks = per // BLOCK
    look = min(-(-DOC_MAX // per), supers - 1)
    groups = width // GROUP
    segs = segments.reshape(-1, LANES)
    skip = skip_gain.reshape(-1, LANES)
    rates, gains = decay_rates.T, residues.T
    any_space = pl.BlockSpec(memory_space=pl.ANY)
    dma = pltpu.SemaphoreType.DMA
    square = (BLOCK, BLOCK)
    vmem = pltpu.VMEM
    return pl.pallas_call(
        functools.partial(fused, n_ctx, n_fsdp, rows, look),
        out_shape=jax.ShapeDtypeStruct((rows, model), BF16),
        in_specs=[any_space] * 6,
        out_specs=pl.BlockSpec(memory_space=vmem),
        scratch_shapes=[
            vmem((3, rows, model), BF16),
            vmem((8, model), BF16),
            vmem((8, model), BF16),
            vmem((8, model), F32),
            vmem(segs.shape, jnp.int32),
            vmem(short_taps.shape, F32),
            vmem((n_fsdp, -(-9 * (short_taps.shape[2] // LANES) // 8) * 8, LANES), F32),
            vmem(rates.shape, F32),
            vmem(rates.shape, F32),
            vmem(skip.shape, F32),
            vmem((8 + per, LANES), F32),
            vmem((members, rows, width), BF16),
            vmem((members, rows, width), BF16),
            vmem((rows, model), BF16),
            vmem((members, rows, width), BF16),
            vmem((members, rows, width), BF16),
            vmem((blocks, lane_tiles, *square), F32),
            vmem((blocks, lane_tiles, *square), F32),
            vmem((lane_tiles, BLOCK, PACK * BLOCK), BF16),
            vmem((lane_tiles, BLOCK, 2 * BLOCK), BF16),
            vmem((lane_tiles, BLOCK, 3 * BLOCK), BF16),
            vmem((lane_tiles, *square), F32),
            vmem((lane_tiles, *square), F32),
            vmem((MODES, width), BF16),
            vmem((look, MODES, width), BF16),
            dma((6,)),
            dma((n_fsdp,)),
            dma((n_fsdp,)),
            dma(()),
            dma(()),
            dma((members,)),
            dma((members,)),
            dma((look,)),
            dma((look,)),
            dma((members,)),
            dma((members,)),
            pltpu.SemaphoreType.REGULAR,
            pltpu.SemaphoreType.REGULAR((max(look - 1, 1),)),
        ],
        compiler_params=pltpu.CompilerParams(
            collective_id=0, has_side_effects=True, vmem_limit_bytes=60 * 1024 * 1024
        ),
    )(streams, segs, short_taps, rates, gains, skip)


def solution(mesh):
    placed = (
        P(None, ("ctx", "fsdp"), None),
        P(),
        P(None, None, "fsdp"),
        P("fsdp", None),
        P("fsdp", None),
        P("fsdp"),
    )
    return jax.shard_map(
        local, mesh=mesh, in_specs=placed, out_specs=P(("ctx", "fsdp"), None), check_vma=False
    )
```

```python
import functools

import jax
import jax.numpy as jnp
from jax import lax
from jax.experimental import pallas as pl
from jax.experimental.pallas import tpu as pltpu
from jax.sharding import PartitionSpec as P

MESH = pl.DeviceIdType.MESH
GROUP = 16
MODES = 16
DOC_MAX = 4096
LANES = 128
BLOCK = 128
PACK = LANES // GROUP
F32 = jnp.float32
BF16 = jnp.bfloat16


def iota(shape, dim):
    return lax.broadcasted_iota(jnp.int32, shape, dim)


def halves(value):
    high = value.astype(BF16)
    return high, (value - high.astype(F32)).astype(BF16)


def one_minus_exp_neg(y):
    total = jnp.ones_like(y)
    for order in range(10, 1, -1):
        total = 1.0 - total * y * (1.0 / order)
    return total * y


def fused(
    n_ctx, n_fsdp, rows, look,
    streams, segs, taps, decay, residue, skip, out,
    x, hs, hb, hf, sg, own_taps, tp, tq, dc, rs, sk, marks, gs, v, qs, ms, mr, inner, fresh, kc, cl, ri, dcy, carry, es, er,
    in_sem, tap_send, tap_recv, tq_send, tq_recv, halo_send, halo_recv, g_send, g_recv, e_send, e_recv, m_send, m_recv, hello, ready,
):
    ctx, f = lax.axis_index("ctx"), lax.axis_index("fsdp")
    supers, members = n_ctx // 2, 2 * n_fsdp
    tile, half = ctx // 2, lax.rem(ctx, 2)
    r = half * n_fsdp + f
    per = members * rows
    blocks = per // BLOCK
    in_block = BLOCK // rows
    width = v.shape[2]
    lane_tiles = width // LANES
    quads = own_taps.shape[2] // LANES

    def member(p):
        return (2 * tile + p // n_fsdp, lax.rem(p, n_fsdp))

    def at_super(step):
        return (ctx + 2 * step, f)

    chip, core = f // 2, lax.rem(f, 2)
    chips = n_fsdp // 2

    def tap_copy(buffer, sends, recvs, owner, to, slot):
        return pltpu.make_async_remote_copy(
            src_ref=buffer.at[owner], dst_ref=buffer.at[owner], send_sem=sends.at[slot],
            recv_sem=recvs.at[owner], device_id=(ctx, to), device_id_type=MESH,
        )

    def kv_taps(owner, to, slot):
        return tap_copy(tp, tap_send, tap_recv, owner, to, slot)

    def query_taps(owner, to, slot):
        return tap_copy(tq, tq_send, tq_recv, owner, to, slot)

    partner = 2 * chip + 1 - core

    def same_core(step):
        return 2 * lax.rem(chip + step, chips) + core

    def other_core(step):
        return 2 * lax.rem(chip + step, chips) + 1 - core

    def spread_taps(copy):
        @pl.loop(1, chips)
        def _(k):
            copy(f, same_core(k), k).start()

        copy(f, partner, 0).start()

    def settle_taps(copy):
        @pl.loop(1, chips)
        def _(k):
            copy(f, same_core(k), k).wait_send()
            copy(same_core(chips - k), partner, chips + k).wait_send()

        copy(f, partner, 0).wait_send()

    more = tile < supers - 1
    sends_halo = more | (r < members - 1)
    gets_halo = (tile > 0) | (r > 0)

    def halo_copy():
        return pltpu.make_async_remote_copy(
            src_ref=hs, dst_ref=hb, send_sem=halo_send, recv_sem=halo_recv,
            device_id=(2 * tile + (r + 1) // n_fsdp, lax.rem(f + 1, n_fsdp)), device_id_type=MESH,
        )

    def block_copy(src, dst, sends, recvs, to, slot):
        return pltpu.make_async_remote_copy(
            src_ref=src.at[to], dst_ref=dst.at[slot], send_sem=sends.at[to],
            recv_sem=recvs.at[slot], device_id=member(to), device_id_type=MESH,
        )

    late = lax.rem(tile, max(supers // 2, 1)) == 0

    def pass_ready(hop, now=True):
        if hop > look:
            return
        known = (tile + hop < supers) & now
        if hop == 1:

            @pl.when((tile > 0) & now)
            def _():
                pl.semaphore_wait(hello, 1)

        else:

            @pl.when(known)
            def _():
                pl.semaphore_wait(ready.at[hop - 2], 1)

        if hop < look:

            @pl.when(known & (tile > 0))
            def _():
                pl.semaphore_signal(
                    ready.at[hop - 1], inc=1, device_id=at_super(-1), device_id_type=MESH
                )

    def state_copy(d):
        return pltpu.make_async_remote_copy(
            src_ref=es, dst_ref=er.at[d - 1], send_sem=e_send.at[d - 1],
            recv_sem=e_recv.at[d - 1], device_id=at_super(d), device_id_type=MESH,
        )

    loads = [
        pltpu.make_async_copy(decay, dc, in_sem.at[0]),
        pltpu.make_async_copy(residue, rs, in_sem.at[1]),
        pltpu.make_async_copy(skip, sk, in_sem.at[2]),
        pltpu.make_async_copy(segs, sg, in_sem.at[3]),
        pltpu.make_async_copy(taps, own_taps, in_sem.at[4]),
        pltpu.make_async_copy(streams, x, in_sem.at[5]),
    ]
    for load in loads:
        load.start()

    barrier = pltpu.get_barrier_semaphore()

    @pl.when(tile > 0)
    def _():
        pl.semaphore_signal(barrier, inc=1, device_id=at_super(-1), device_id_type=MESH)

    @pl.when((tile > 0) & (r == 0))
    def _():
        pl.semaphore_signal(
            barrier, inc=1, device_id=(2 * tile - 1, n_fsdp - 1), device_id_type=MESH
        )

    @pl.loop(0, members)
    def _(k):
        to = lax.rem(r + n_fsdp + k, members)

        @pl.when(to != r)
        def _():
            pl.semaphore_signal(barrier, inc=1, device_id=member(to), device_id_type=MESH)

    loads[4].wait()
    for s in range(3):
        for j in range(3):
            for q in range(quads):
                row = (max(s - 1, 0) * 3 + j) * quads + q
                line = own_taps[s, j : j + 1, q * LANES : (q + 1) * LANES]
                if s == 0:
                    tq[f, row : row + 1, :] = line
                else:
                    tp[f, row : row + 1, :] = line

    greets = jnp.where(more, 1, 0) + jnp.where(more & (r == members - 1), 1, 0)
    pl.semaphore_wait(barrier, members - 1 + greets)

    spread_taps(kv_taps)

    loads[5].wait()
    step = 4 * LANES
    slot = iota((8, step), 0) // 2

    @pl.loop(0, x.shape[2] // step)
    def _(k):
        col = pl.ds(pl.multiple_of(k * step, step), step)
        total = jnp.zeros((8, step), F32)
        for s in range(3):
            tail = x[s, rows - 8 : rows, col].astype(F32)
            total = jnp.where(slot == s, pltpu.roll(tail, 2 * s + 2, 0), total)
        hs[:, col] = total.astype(BF16)

    @pl.when(sends_halo)
    def _():
        halo_copy().start()

    @pl.when(more)
    def _():
        pl.semaphore_signal(hello, inc=1, device_id=at_super(1), device_id_type=MESH)

    pass_ready(1, jnp.logical_not(late))

    for load in loads[:4]:
        load.wait()
    square = (BLOCK, BLOCK)
    down, across = iota(square, 0), iota(square, 1)
    eye = down == across
    causal = down >= across
    same_group = (down // MODES) == (across // GROUP)
    away = lax.rem(BLOCK - across, BLOCK).astype(F32)

    def to_column(row):
        return jnp.sum(jnp.where(eye, jnp.broadcast_to(row, square), 0.0), axis=1, keepdims=True)

    def mark_row(index):
        return sg[pl.ds(index, 1), :].astype(F32)

    rates = dc[...]
    gains = rs[...] * jnp.sqrt(one_minus_exp_neg(2.0 * rates))
    for m in range(lane_tiles):
        base = half * (lane_tiles * PACK) + m * PACK
        own = iota((BLOCK, rates.shape[1]), 1) == base + iota((BLOCK, rates.shape[1]), 0) // MODES

        def spread(small):
            tall = jnp.concatenate([small] * PACK, axis=0)
            return jnp.sum(jnp.where(own, tall, 0.0), axis=1, keepdims=True)

        rate = jnp.broadcast_to(spread(rates), square)
        gain = jnp.broadcast_to(spread(gains), square)
        rate_row = jnp.sum(jnp.where(eye, rate, 0.0), axis=0, keepdims=True)
        gain_row = jnp.sum(jnp.where(eye, gain, 0.0), axis=0, keepdims=True)
        dcy[m] = rate
        rise = gain_row * jnp.exp(-rate_row * (down + 1).astype(F32))
        high, low = halves(rise)
        ri[m] = jnp.concatenate([high, low, high], axis=1)
        close = jnp.exp(-rate * (BLOCK - 1 - across).astype(F32))
        high, low = halves(close)
        cl[m] = jnp.concatenate([high, low], axis=1)
        taps_of = jnp.sum(
            (gain * jnp.exp(-rate * away)).reshape(PACK, MODES, BLOCK), axis=1
        )
        for g in range(PACK):
            line = jnp.broadcast_to(taps_of[g : g + 1, :], square)
            line = pltpu.roll(line, 0, 1, stride=1, stride_axis=0)
            kc[m, :, g * BLOCK : (g + 1) * BLOCK] = jnp.where(causal, line, 0.0).astype(BF16)

    top = tile * blocks
    before_row = mark_row(jnp.maximum(top - 1, 0))
    before_col = to_column(before_row)[BLOCK - 8 :]
    before_col = jnp.where(tile > 0, before_col, -1.0)
    marks[0:8, :] = jnp.broadcast_to(before_col, (8, LANES))
    for b in range(blocks):
        marks[8 + b * BLOCK : 8 + (b + 1) * BLOCK, :] = jnp.broadcast_to(
            to_column(mark_row(top + b)), square
        )

    @pl.when(gets_halo)
    def _():
        halo_copy().wait_recv()
        hf[...] = hb[...].astype(F32)

    @pl.when(jnp.logical_not(gets_halo))
    def _():
        hf[...] = jnp.zeros_like(hf)

    pass_ready(1, late)

    window = marks[pl.ds(pl.multiple_of(r * rows, rows), rows + 8), :]
    own_marks = window[8:]
    agree = [None] + [window[8 - j : 8 - j + rows] == own_marks for j in (1, 2)]
    row_id = iota((rows, LANES), 0)

    def feature(s, owner, lane, chunk):
        col = pl.ds(pl.multiple_of(chunk * LANES, LANES), LANES)
        now = x[s, :, col].astype(F32)
        prev1 = hf[2 * s + 1 : 2 * s + 2, col]
        prev2 = hf[2 * s : 2 * s + 1, col]
        shift1 = jnp.where(row_id == 0, prev1, pltpu.roll(now, 1, 0))
        shift2 = jnp.where(row_id == 0, prev2, jnp.where(row_id == 1, prev1, pltpu.roll(now, 2, 0)))

        def tap(j):
            row = (max(s - 1, 0) * 3 + j) * quads + lane
            return (tp if s else tq)[owner, pl.ds(row, 1), :]

        total = now * tap(0)
        total = total + jnp.where(agree[1], shift1, 0.0) * tap(1)
        return total + jnp.where(agree[2], shift2, 0.0) * tap(2)

    def chunk_of(owner, lane):
        chunk = owner * (2 * lane_tiles) + lane
        return chunk, pl.ds(pl.multiple_of(chunk * LANES, LANES), LANES)

    def send_gated(owner, part):
        to = part * n_fsdp + owner
        for m in range(lane_tiles):
            lane = part * lane_tiles + m
            chunk, _ = chunk_of(owner, lane)
            gated = feature(1, owner, lane, chunk) * feature(2, owner, lane, chunk)
            gs[to, :, m * LANES : (m + 1) * LANES] = gated.astype(BF16)

        @pl.when(to != r)
        def _():
            block_copy(gs, v, g_send, g_recv, to, r).start()

    far_half, near_half = 1 - half, half
    send_gated(f, far_half)
    pass_ready(2)

    @pl.loop(1, chips)
    def _(k):
        owner = same_core(chips - k)
        kv_taps(owner, partner, chips + k).wait_recv()
        kv_taps(owner, partner, chips + k).start()
        send_gated(owner, far_half)

    pass_ready(3)

    @pl.loop(0, chips)
    def _(k):
        owner = other_core(chips - k)
        kv_taps(owner, f, 0).wait_recv()
        send_gated(owner, far_half)

    @pl.loop(0, n_fsdp)
    def _(k):
        send_gated(lax.rem(f + n_fsdp - k, n_fsdp), near_half)

    spread_taps(query_taps)
    v[r] = gs[r]

    def marks_of(b):
        return marks[8 + b * BLOCK : 8 + (b + 1) * BLOCK, :]

    def end_mark(b):
        if b < 0:
            return marks[7:8, :]
        return marks[7 + (b + 1) * BLOCK : 8 + (b + 1) * BLOCK, :]

    def values(b, m):
        four = v[b * in_block : (b + 1) * in_block, :, m * LANES : (m + 1) * LANES]
        return four.reshape(BLOCK, LANES)

    spot = same_group.astype(F32)
    for b in range(blocks):
        for p in range(b * in_block, (b + 1) * in_block):

            @pl.when(r != p)
            def _(p=p):
                block_copy(gs, v, g_send, g_recv, r, p).wait_recv()

        ending = (marks_of(b) == end_mark(b)).astype(F32)
        for m in range(lane_tiles):
            kept = (values(b, m).astype(F32) * ending).astype(BF16)
            fresh[b, m] = spot * jnp.dot(
                cl[m], jnp.concatenate([kept, kept], axis=0), preferred_element_type=F32
            )

    for m in range(lane_tiles):
        fade = jnp.exp(-dcy[m] * float(BLOCK))
        state = fresh[0, m]
        for b in range(1, blocks):
            passing = (end_mark(b) == end_mark(b - 1)).astype(F32)
            state = passing * fade * state + fresh[b, m]
        es[:, m * LANES : (m + 1) * LANES] = jnp.sum(
            state.reshape(PACK, MODES, LANES), axis=0
        ).astype(BF16)
    for hop in range(4, look + 1):
        pass_ready(hop)
    for d in range(look, 0, -1):

        @pl.when(tile + d < supers)
        def _(d=d):
            state_copy(d).start()


    lane_group = iota((1, LANES), 1) // GROUP
    for b in range(blocks):
        row = jnp.broadcast_to(mark_row(top + b), square)
        agreeing = (marks_of(b) == row).astype(BF16)
        agreeing = jnp.concatenate([agreeing] * PACK, axis=1)
        for m in range(lane_tiles):
            vals = values(b, m)
            parts = [vals * (lane_group == g).astype(BF16) for g in range(PACK)]
            direct = jnp.dot(
                kc[m] * agreeing, jnp.concatenate(parts, axis=0), preferred_element_type=F32
            )
            gain = sk[pl.ds(half * lane_tiles + m, 1), :]
            inner[b, m] = direct + gain * vals.astype(F32)

    @pl.loop(1, chips)
    def _(k):
        owner = same_core(chips - k)
        query_taps(owner, partner, chips + k).wait_recv()
        query_taps(owner, partner, chips + k).start()

    def make_queries(owner):
        for lane in range(2 * lane_tiles):
            chunk, col = chunk_of(owner, lane)
            qs[:, col] = feature(0, owner, lane, chunk).astype(BF16)

    make_queries(f)

    @pl.loop(1, chips)
    def _(k):
        make_queries(same_core(chips - k))

    @pl.loop(0, chips)
    def _(k):
        owner = other_core(chips - k)
        query_taps(owner, f, 0).wait_recv()
        make_queries(owner)

    def brought(m, state):
        high, low = halves(state)
        return jnp.dot(
            ri[m], jnp.concatenate([high, high, low], axis=0), preferred_element_type=F32
        )

    for m in range(lane_tiles):
        fade = jnp.exp(-dcy[m] * float(BLOCK))
        state = fresh[0, m]
        factor = jnp.ones(square, F32)
        fresh[0, m] = factor
        for b in range(1, blocks):
            follow = (marks_of(b) == end_mark(b - 1)).astype(F32)
            inner[b, m] += follow * brought(m, state)
            if b < blocks - 1:
                passing = (end_mark(b) == end_mark(b - 1)).astype(F32)
                state = passing * fade * state + fresh[b, m]
            passed = (end_mark(b - 1) == end_mark(b - 2)).astype(F32)
            factor = passed * fade * factor
            fresh[b, m] = factor

    first_mark = marks[8:9, :]
    for m in range(lane_tiles):
        carry[m] = jnp.zeros(square, F32)
    for d in range(1, look + 1):

        @pl.when(tile >= d)
        def _(d=d):
            state_copy(d).wait_recv()
            its_end = mark_row((tile - d) * blocks + blocks - 1)[:, LANES - 1 :]
            joined = spot * (jnp.broadcast_to(its_end, (1, LANES)) == first_mark).astype(F32)
            for m in range(lane_tiles):
                part = er[d - 1, :, m * LANES : (m + 1) * LANES].astype(F32)
                part = joined * jnp.concatenate([part] * PACK, axis=0)
                if d > 1:
                    part = part * jnp.exp(-dcy[m] * float(per * (d - 1)))
                carry[m] += part

    @pl.loop(0, blocks)
    def _(k):
        b = lax.rem(r // in_block + blocks // 2 + k, blocks)
        start = pl.multiple_of(b * BLOCK, BLOCK)
        follow = (marks[pl.ds(start + 8, BLOCK), :] == marks[pl.ds(start, 8), :][7:]).astype(F32)
        for m in range(lane_tiles):
            mixed = (inner[b, m] + follow * brought(m, carry[m] * fresh[b, m])).astype(BF16)
            ms[pl.ds(b * in_block, in_block), :, m * LANES : (m + 1) * LANES] = mixed.reshape(
                in_block, rows, LANES
            )
        for q in range(in_block):
            to = b * in_block + q

            @pl.when(r != to)
            def _(to=to):
                block_copy(ms, mr, m_send, m_recv, to, r).start()

    mr[r] = ms[r]

    @pl.loop(0, members)
    def _(k):
        source = lax.rem(r + members - k, members)

        @pl.when(k > 0)
        def _():
            block_copy(ms, mr, m_send, m_recv, r, source).wait_recv()

        base = lax.rem(source, n_fsdp) * (2 * width) + (source // n_fsdp) * width
        col = pl.ds(pl.multiple_of(base, width), width)
        out[:, col] = (qs[:, col].astype(F32) * mr[source].astype(F32)).astype(BF16)

    @pl.when(sends_halo)
    def _():
        halo_copy().wait_send()

    settle_taps(kv_taps)
    settle_taps(query_taps)

    @pl.loop(1, members)
    def _(k):
        to = lax.rem(r + k, members)
        block_copy(gs, v, g_send, g_recv, to, r).wait_send()
        block_copy(ms, mr, m_send, m_recv, to, r).wait_send()

    for d in range(1, look + 1):

        @pl.when(tile + d < supers)
        def _(d=d):
            state_copy(d).wait_send()


def local(streams, segments, short_taps, decay_rates, residues, skip_gain):
    n_ctx, n_fsdp = lax.axis_size("ctx"), lax.axis_size("fsdp")
    rows, model = streams.shape[1:]
    supers, members = n_ctx // 2, 2 * n_fsdp
    width = model // members
    lane_tiles = width // LANES
    per = members * rows
    blocks = per // BLOCK
    look = min(-(-DOC_MAX // per), supers - 1)
    groups = width // GROUP
    segs = segments.reshape(-1, LANES)
    skip = skip_gain.reshape(-1, LANES)
    rates, gains = decay_rates.T, residues.T
    any_space = pl.BlockSpec(memory_space=pl.ANY)
    dma = pltpu.SemaphoreType.DMA
    square = (BLOCK, BLOCK)
    vmem = pltpu.VMEM
    return pl.pallas_call(
        functools.partial(fused, n_ctx, n_fsdp, rows, look),
        out_shape=vmem((rows, model), BF16),
        in_specs=[any_space] * 6,
        out_specs=pl.BlockSpec(memory_space=vmem),
        scratch_shapes=[
            vmem((3, rows, model), BF16),
            vmem((8, model), BF16),
            vmem((8, model), BF16),
            vmem((8, model), F32),
            vmem(segs.shape, jnp.int32),
            vmem(short_taps.shape, F32),
            vmem((n_fsdp, 6 * (short_taps.shape[2] // LANES), LANES), F32),
            vmem((n_fsdp, 4 * (short_taps.shape[2] // LANES), LANES), F32),
            vmem(rates.shape, F32),
            vmem(rates.shape, F32),
            vmem(skip.shape, F32),
            vmem((8 + per, LANES), F32),
            vmem((members, rows, width), BF16),
            vmem((members, rows, width), BF16),
            vmem((rows, model), BF16),
            vmem((members, rows, width), BF16),
            vmem((members, rows, width), BF16),
            vmem((blocks, lane_tiles, *square), F32),
            vmem((blocks, lane_tiles, *square), F32),
            vmem((lane_tiles, BLOCK, PACK * BLOCK), BF16),
            vmem((lane_tiles, BLOCK, 2 * BLOCK), BF16),
            vmem((lane_tiles, BLOCK, 3 * BLOCK), BF16),
            vmem((lane_tiles, *square), F32),
            vmem((lane_tiles, *square), F32),
            vmem((MODES, width), BF16),
            vmem((look, MODES, width), BF16),
            dma((6,)),
            dma((n_fsdp,)),
            dma((n_fsdp,)),
            dma((n_fsdp,)),
            dma((n_fsdp,)),
            dma(()),
            dma(()),
            dma((members,)),
            dma((members,)),
            dma((look,)),
            dma((look,)),
            dma((members,)),
            dma((members,)),
            pltpu.SemaphoreType.REGULAR,
            pltpu.SemaphoreType.REGULAR((max(look - 1, 1),)),
        ],
        compiler_params=pltpu.CompilerParams(
            collective_id=0, has_side_effects=True, vmem_limit_bytes=60 * 1024 * 1024
        ),
    )(streams, segs, short_taps, rates, gains, skip)


def solution(mesh):
    placed = (
        P(None, ("ctx", "fsdp"), None),
        P(),
        P(None, None, "fsdp"),
        P("fsdp", None),
        P("fsdp", None),
        P("fsdp"),
    )
    return jax.shard_map(
        local, mesh=mesh, in_specs=placed, out_specs=P(("ctx", "fsdp"), None), check_vma=False
    )
```

```python
import functools

import jax
import jax.numpy as jnp
from jax import lax
from jax.experimental import pallas as pl
from jax.experimental.pallas import tpu as pltpu
from jax.sharding import PartitionSpec as P

MESH = pl.DeviceIdType.MESH
GROUP = 16
MODES = 16
DOC_MAX = 4096
LANES = 128
BLOCK = 128
PACK = LANES // GROUP
F32 = jnp.float32
BF16 = jnp.bfloat16


def iota(shape, dim):
    return lax.broadcasted_iota(jnp.int32, shape, dim)


def halves(value):
    high = value.astype(BF16)
    return high, (value - high.astype(F32)).astype(BF16)


def one_minus_exp_neg(y):
    total = jnp.ones_like(y)
    for order in range(10, 1, -1):
        total = 1.0 - total * y * (1.0 / order)
    return total * y


def fused(
    n_ctx, n_fsdp, rows, look,
    streams, segs, taps, decay, residue, skip, out,
    x, qhs, hs, qhb, hb, hf, sg, own_taps, tp, tq, dc, rs, sk, marks, gs, v, qs, ms, mr, inner, fresh, kc, cl, ri, dcy, carry, es, er,
    in_sem, tap_send, tap_recv, tq_send, tq_recv, halo_send, halo_recv, g_send, g_recv, e_send, e_recv, m_send, m_recv, hello, ready,
):
    ctx, f = lax.axis_index("ctx"), lax.axis_index("fsdp")
    supers, members = n_ctx // 2, 2 * n_fsdp
    tile, half = ctx // 2, lax.rem(ctx, 2)
    r = half * n_fsdp + f
    per = members * rows
    blocks = per // BLOCK
    in_block = BLOCK // rows
    width = v.shape[2]
    lane_tiles = width // LANES
    quads = own_taps.shape[2] // LANES

    def member(p):
        return (2 * tile + p // n_fsdp, lax.rem(p, n_fsdp))

    def at_super(step):
        return (ctx + 2 * step, f)

    chip, core = f // 2, lax.rem(f, 2)
    chips = n_fsdp // 2

    def tap_copy(buffer, sends, recvs, owner, to, slot):
        return pltpu.make_async_remote_copy(
            src_ref=buffer.at[owner], dst_ref=buffer.at[owner], send_sem=sends.at[slot],
            recv_sem=recvs.at[owner], device_id=(ctx, to), device_id_type=MESH,
        )

    def kv_taps(owner, to, slot):
        return tap_copy(tp, tap_send, tap_recv, owner, to, slot)

    def query_taps(owner, to, slot):
        return tap_copy(tq, tq_send, tq_recv, owner, to, slot)

    partner = 2 * chip + 1 - core

    def same_core(step):
        return 2 * lax.rem(chip + step, chips) + core

    def other_core(step):
        return 2 * lax.rem(chip + step, chips) + 1 - core

    def spread_taps(copy):
        @pl.loop(1, chips)
        def _(k):
            copy(f, same_core(k), k).start()

        copy(f, partner, 0).start()

    def settle_taps(copy):
        @pl.loop(1, chips)
        def _(k):
            copy(f, same_core(k), k).wait_send()
            copy(same_core(chips - k), partner, chips + k).wait_send()

        copy(f, partner, 0).wait_send()

    more = tile < supers - 1
    sends_halo = more | (r < members - 1)
    gets_halo = (tile > 0) | (r > 0)

    def halo_copy(part=1):
        return pltpu.make_async_remote_copy(
            src_ref=hs if part else qhs, dst_ref=hb if part else qhb,
            send_sem=halo_send.at[part], recv_sem=halo_recv.at[part],
            device_id=(2 * tile + (r + 1) // n_fsdp, lax.rem(f + 1, n_fsdp)), device_id_type=MESH,
        )

    def block_copy(src, dst, sends, recvs, to, slot):
        return pltpu.make_async_remote_copy(
            src_ref=src.at[to], dst_ref=dst.at[slot], send_sem=sends.at[to],
            recv_sem=recvs.at[slot], device_id=member(to), device_id_type=MESH,
        )

    late = lax.rem(tile, max(supers // 2, 1)) == 0

    def pass_ready(hop, now=True):
        if hop > look:
            return
        known = (tile + hop < supers) & now
        if hop == 1:

            @pl.when((tile > 0) & now)
            def _():
                pl.semaphore_wait(hello, 1)

        else:

            @pl.when(known)
            def _():
                pl.semaphore_wait(ready.at[hop - 2], 1)

        if hop < look:

            @pl.when(known & (tile > 0))
            def _():
                pl.semaphore_signal(
                    ready.at[hop - 1], inc=1, device_id=at_super(-1), device_id_type=MESH
                )

    def state_copy(d):
        return pltpu.make_async_remote_copy(
            src_ref=es, dst_ref=er.at[d - 1], send_sem=e_send.at[d - 1],
            recv_sem=e_recv.at[d - 1], device_id=at_super(d), device_id_type=MESH,
        )

    loads = [
        pltpu.make_async_copy(decay, dc, in_sem.at[0]),
        pltpu.make_async_copy(residue, rs, in_sem.at[1]),
        pltpu.make_async_copy(skip, sk, in_sem.at[2]),
        pltpu.make_async_copy(segs, sg, in_sem.at[3]),
        pltpu.make_async_copy(taps, own_taps, in_sem.at[4]),
        pltpu.make_async_copy(streams, x, in_sem.at[5]),
    ]
    for load in loads:
        load.start()

    barrier = pltpu.get_barrier_semaphore()

    @pl.when(tile > 0)
    def _():
        pl.semaphore_signal(barrier, inc=1, device_id=at_super(-1), device_id_type=MESH)

    @pl.when((tile > 0) & (r == 0))
    def _():
        pl.semaphore_signal(
            barrier, inc=1, device_id=(2 * tile - 1, n_fsdp - 1), device_id_type=MESH
        )

    @pl.loop(0, members)
    def _(k):
        to = lax.rem(r + n_fsdp + k, members)

        @pl.when(to != r)
        def _():
            pl.semaphore_signal(barrier, inc=1, device_id=member(to), device_id_type=MESH)

    loads[4].wait()
    for s in range(3):
        for j in range(3):
            for q in range(quads):
                row = (max(s - 1, 0) * 3 + j) * quads + q
                line = own_taps[s, j : j + 1, q * LANES : (q + 1) * LANES]
                if s == 0:
                    tq[f, row : row + 1, :] = line
                else:
                    tp[f, row : row + 1, :] = line

    greets = jnp.where(more, 1, 0) + jnp.where(more & (r == members - 1), 1, 0)
    pl.semaphore_wait(barrier, members - 1 + greets)

    spread_taps(kv_taps)

    loads[5].wait()
    step = 4 * LANES
    slot = iota((8, step), 0) // 2

    @pl.loop(0, x.shape[2] // step)
    def _(k):
        col = pl.ds(pl.multiple_of(k * step, step), step)
        total = jnp.zeros((8, step), F32)
        for s in range(3):
            tail = x[s, rows - 8 : rows, col].astype(F32)
            total = jnp.where(slot == s, pltpu.roll(tail, 2 * s + 2, 0), total)
        qhs[:, col] = total[:2].astype(BF16)
        hs[:, col] = total[2:6].astype(BF16)

    @pl.when(sends_halo)
    def _():
        halo_copy().start()

    @pl.when(more)
    def _():
        pl.semaphore_signal(hello, inc=1, device_id=at_super(1), device_id_type=MESH)

    pass_ready(1, jnp.logical_not(late))

    for load in loads[:4]:
        load.wait()
    square = (BLOCK, BLOCK)
    down, across = iota(square, 0), iota(square, 1)
    eye = down == across
    causal = down >= across
    same_group = (down // MODES) == (across // GROUP)
    away = lax.rem(BLOCK - across, BLOCK).astype(F32)

    def to_column(row):
        return jnp.sum(jnp.where(eye, jnp.broadcast_to(row, square), 0.0), axis=1, keepdims=True)

    def mark_row(index):
        return sg[pl.ds(index, 1), :].astype(F32)

    rates = dc[...]
    gains = rs[...] * jnp.sqrt(one_minus_exp_neg(2.0 * rates))
    for m in range(lane_tiles):
        base = half * (lane_tiles * PACK) + m * PACK
        own = iota((BLOCK, rates.shape[1]), 1) == base + iota((BLOCK, rates.shape[1]), 0) // MODES

        def spread(small):
            tall = jnp.concatenate([small] * PACK, axis=0)
            return jnp.sum(jnp.where(own, tall, 0.0), axis=1, keepdims=True)

        rate = jnp.broadcast_to(spread(rates), square)
        gain = jnp.broadcast_to(spread(gains), square)
        rate_row = jnp.sum(jnp.where(eye, rate, 0.0), axis=0, keepdims=True)
        gain_row = jnp.sum(jnp.where(eye, gain, 0.0), axis=0, keepdims=True)
        dcy[m] = rate
        rise = gain_row * jnp.exp(-rate_row * (down + 1).astype(F32))
        high, low = halves(rise)
        ri[m] = jnp.concatenate([high, low, high], axis=1)
        close = jnp.exp(-rate * (BLOCK - 1 - across).astype(F32))
        high, low = halves(close)
        cl[m] = jnp.concatenate([high, low], axis=1)
        taps_of = jnp.sum(
            (gain * jnp.exp(-rate * away)).reshape(PACK, MODES, BLOCK), axis=1
        )
        for g in range(PACK):
            line = jnp.broadcast_to(taps_of[g : g + 1, :], square)
            line = pltpu.roll(line, 0, 1, stride=1, stride_axis=0)
            kc[m, :, g * BLOCK : (g + 1) * BLOCK] = jnp.where(causal, line, 0.0).astype(BF16)

    top = tile * blocks
    before_row = mark_row(jnp.maximum(top - 1, 0))
    before_col = to_column(before_row)[BLOCK - 8 :]
    before_col = jnp.where(tile > 0, before_col, -1.0)
    marks[0:8, :] = jnp.broadcast_to(before_col, (8, LANES))
    for b in range(blocks):
        marks[8 + b * BLOCK : 8 + (b + 1) * BLOCK, :] = jnp.broadcast_to(
            to_column(mark_row(top + b)), square
        )

    @pl.when(gets_halo)
    def _():
        halo_copy().wait_recv()
        hf[2:6, :] = hb[...].astype(F32)

    @pl.when(jnp.logical_not(gets_halo))
    def _():
        hf[...] = jnp.zeros_like(hf)

    pass_ready(1, late)

    window = marks[pl.ds(pl.multiple_of(r * rows, rows), rows + 8), :]
    own_marks = window[8:]
    agree = [None] + [window[8 - j : 8 - j + rows] == own_marks for j in (1, 2)]
    row_id = iota((rows, LANES), 0)

    def feature(s, owner, lane, chunk):
        col = pl.ds(pl.multiple_of(chunk * LANES, LANES), LANES)
        now = x[s, :, col].astype(F32)
        prev1 = hf[2 * s + 1 : 2 * s + 2, col]
        prev2 = hf[2 * s : 2 * s + 1, col]
        shift1 = jnp.where(row_id == 0, prev1, pltpu.roll(now, 1, 0))
        shift2 = jnp.where(row_id == 0, prev2, jnp.where(row_id == 1, prev1, pltpu.roll(now, 2, 0)))

        def tap(j):
            row = (max(s - 1, 0) * 3 + j) * quads + lane
            return (tp if s else tq)[owner, pl.ds(row, 1), :]

        total = now * tap(0)
        total = total + jnp.where(agree[1], shift1, 0.0) * tap(1)
        return total + jnp.where(agree[2], shift2, 0.0) * tap(2)

    def chunk_of(owner, lane):
        chunk = owner * (2 * lane_tiles) + lane
        return chunk, pl.ds(pl.multiple_of(chunk * LANES, LANES), LANES)

    def send_gated(owner, part):
        to = part * n_fsdp + owner
        for m in range(lane_tiles):
            lane = part * lane_tiles + m
            chunk, _ = chunk_of(owner, lane)
            gated = feature(1, owner, lane, chunk) * feature(2, owner, lane, chunk)
            gs[to, :, m * LANES : (m + 1) * LANES] = gated.astype(BF16)

        @pl.when(to != r)
        def _():
            block_copy(gs, v, g_send, g_recv, to, r).start()

    far_half, near_half = 1 - half, half
    send_gated(f, far_half)
    pass_ready(2)

    @pl.loop(1, chips)
    def _(k):
        owner = same_core(chips - k)
        kv_taps(owner, partner, chips + k).wait_recv()
        kv_taps(owner, partner, chips + k).start()
        send_gated(owner, far_half)

    pass_ready(3)

    @pl.loop(0, chips)
    def _(k):
        owner = other_core(chips - k)
        kv_taps(owner, f, 0).wait_recv()
        send_gated(owner, far_half)

    @pl.loop(0, n_fsdp)
    def _(k):
        send_gated(lax.rem(f + n_fsdp - k, n_fsdp), near_half)

    @pl.when(sends_halo)
    def _():
        halo_copy(0).start()

    spread_taps(query_taps)
    v[r] = gs[r]

    def marks_of(b):
        return marks[8 + b * BLOCK : 8 + (b + 1) * BLOCK, :]

    def end_mark(b):
        if b < 0:
            return marks[7:8, :]
        return marks[7 + (b + 1) * BLOCK : 8 + (b + 1) * BLOCK, :]

    def values(b, m):
        four = v[b * in_block : (b + 1) * in_block, :, m * LANES : (m + 1) * LANES]
        return four.reshape(BLOCK, LANES)

    spot = same_group.astype(F32)

    @pl.loop(0, blocks)
    def _(k):
        b = lax.rem(far_half * (blocks // 2) + k, blocks)
        for q in range(in_block):
            source = b * in_block + q

            @pl.when(r != source)
            def _(source=source):
                block_copy(gs, v, g_send, g_recv, r, source).wait_recv()

        start = pl.multiple_of(b * BLOCK, BLOCK)
        its_end = marks[pl.ds(start + BLOCK, 8), :][7:]
        ending = (marks[pl.ds(start + 8, BLOCK), :] == its_end).astype(F32)
        for m in range(lane_tiles):
            four = v[pl.ds(b * in_block, in_block), :, m * LANES : (m + 1) * LANES]
            kept = (four.reshape(BLOCK, LANES).astype(F32) * ending).astype(BF16)
            fresh[b, m] = spot * jnp.dot(
                cl[m], jnp.concatenate([kept, kept], axis=0), preferred_element_type=F32
            )

    for m in range(lane_tiles):
        fade = jnp.exp(-dcy[m] * float(BLOCK))
        state = fresh[0, m]
        for b in range(1, blocks):
            passing = (end_mark(b) == end_mark(b - 1)).astype(F32)
            state = passing * fade * state + fresh[b, m]
        es[:, m * LANES : (m + 1) * LANES] = jnp.sum(
            state.reshape(PACK, MODES, LANES), axis=0
        ).astype(BF16)
    for hop in range(4, look + 1):
        pass_ready(hop)
    for d in range(look, 0, -1):

        @pl.when(tile + d < supers)
        def _(d=d):
            state_copy(d).start()


    lane_group = iota((1, LANES), 1) // GROUP
    for b in range(blocks):
        row = jnp.broadcast_to(mark_row(top + b), square)
        agreeing = (marks_of(b) == row).astype(BF16)
        agreeing = jnp.concatenate([agreeing] * PACK, axis=1)
        for m in range(lane_tiles):
            vals = values(b, m)
            parts = [vals * (lane_group == g).astype(BF16) for g in range(PACK)]
            direct = jnp.dot(
                kc[m] * agreeing, jnp.concatenate(parts, axis=0), preferred_element_type=F32
            )
            gain = sk[pl.ds(half * lane_tiles + m, 1), :]
            inner[b, m] = direct + gain * vals.astype(F32)

    @pl.loop(1, chips)
    def _(k):
        owner = same_core(chips - k)
        query_taps(owner, partner, chips + k).wait_recv()
        query_taps(owner, partner, chips + k).start()

    def make_queries(owner):
        for lane in range(2 * lane_tiles):
            chunk, col = chunk_of(owner, lane)
            qs[:, col] = feature(0, owner, lane, chunk).astype(BF16)

    @pl.when(gets_halo)
    def _():
        halo_copy(0).wait_recv()
        hf[0:2, :] = qhb[...].astype(F32)

    make_queries(f)

    @pl.loop(1, chips)
    def _(k):
        make_queries(same_core(chips - k))

    @pl.loop(0, chips)
    def _(k):
        owner = other_core(chips - k)
        query_taps(owner, f, 0).wait_recv()
        make_queries(owner)

    def brought(m, state):
        high, low = halves(state)
        return jnp.dot(
            ri[m], jnp.concatenate([high, high, low], axis=0), preferred_element_type=F32
        )

    for m in range(lane_tiles):
        fade = jnp.exp(-dcy[m] * float(BLOCK))
        state = fresh[0, m]
        factor = jnp.ones(square, F32)
        fresh[0, m] = factor
        for b in range(1, blocks):
            follow = (marks_of(b) == end_mark(b - 1)).astype(F32)
            inner[b, m] += follow * brought(m, state)
            if b < blocks - 1:
                passing = (end_mark(b) == end_mark(b - 1)).astype(F32)
                state = passing * fade * state + fresh[b, m]
            passed = (end_mark(b - 1) == end_mark(b - 2)).astype(F32)
            factor = passed * fade * factor
            fresh[b, m] = factor

    first_mark = marks[8:9, :]
    for m in range(lane_tiles):
        carry[m] = jnp.zeros(square, F32)
    for d in range(1, look + 1):

        @pl.when(tile >= d)
        def _(d=d):
            state_copy(d).wait_recv()
            its_end = mark_row((tile - d) * blocks + blocks - 1)[:, LANES - 1 :]
            joined = spot * (jnp.broadcast_to(its_end, (1, LANES)) == first_mark).astype(F32)
            for m in range(lane_tiles):
                part = er[d - 1, :, m * LANES : (m + 1) * LANES].astype(F32)
                part = joined * jnp.concatenate([part] * PACK, axis=0)
                if d > 1:
                    part = part * jnp.exp(-dcy[m] * float(per * (d - 1)))
                carry[m] += part

    @pl.loop(0, blocks)
    def _(k):
        b = lax.rem(r // in_block + blocks // 2 + k, blocks)
        start = pl.multiple_of(b * BLOCK, BLOCK)
        follow = (marks[pl.ds(start + 8, BLOCK), :] == marks[pl.ds(start, 8), :][7:]).astype(F32)
        for m in range(lane_tiles):
            mixed = (inner[b, m] + follow * brought(m, carry[m] * fresh[b, m])).astype(BF16)
            ms[pl.ds(b * in_block, in_block), :, m * LANES : (m + 1) * LANES] = mixed.reshape(
                in_block, rows, LANES
            )
        for q in range(in_block):
            to = b * in_block + q

            @pl.when(r != to)
            def _(to=to):
                block_copy(ms, mr, m_send, m_recv, to, r).start()

    mr[r] = ms[r]

    @pl.loop(0, members)
    def _(k):
        source = lax.rem(r + members + n_fsdp - k, members)

        @pl.when(source != r)
        def _():
            block_copy(ms, mr, m_send, m_recv, r, source).wait_recv()

        base = lax.rem(source, n_fsdp) * (2 * width) + (source // n_fsdp) * width
        col = pl.ds(pl.multiple_of(base, width), width)
        out[:, col] = (qs[:, col].astype(F32) * mr[source].astype(F32)).astype(BF16)

    @pl.when(sends_halo)
    def _():
        halo_copy(0).wait_send()
        halo_copy(1).wait_send()

    settle_taps(kv_taps)
    settle_taps(query_taps)

    @pl.loop(1, members)
    def _(k):
        to = lax.rem(r + k, members)
        block_copy(gs, v, g_send, g_recv, to, r).wait_send()
        block_copy(ms, mr, m_send, m_recv, to, r).wait_send()

    for d in range(1, look + 1):

        @pl.when(tile + d < supers)
        def _(d=d):
            state_copy(d).wait_send()


def local(streams, segments, short_taps, decay_rates, residues, skip_gain):
    n_ctx, n_fsdp = lax.axis_size("ctx"), lax.axis_size("fsdp")
    rows, model = streams.shape[1:]
    supers, members = n_ctx // 2, 2 * n_fsdp
    width = model // members
    lane_tiles = width // LANES
    per = members * rows
    blocks = per // BLOCK
    look = min(-(-DOC_MAX // per), supers - 1)
    groups = width // GROUP
    segs = segments.reshape(-1, LANES)
    skip = skip_gain.reshape(-1, LANES)
    rates, gains = decay_rates.T, residues.T
    any_space = pl.BlockSpec(memory_space=pl.ANY)
    dma = pltpu.SemaphoreType.DMA
    square = (BLOCK, BLOCK)
    vmem = pltpu.VMEM
    return pl.pallas_call(
        functools.partial(fused, n_ctx, n_fsdp, rows, look),
        out_shape=vmem((rows, model), BF16),
        in_specs=[any_space] * 6,
        out_specs=pl.BlockSpec(memory_space=vmem),
        scratch_shapes=[
            vmem((3, rows, model), BF16),
            vmem((2, model), BF16),
            vmem((4, model), BF16),
            vmem((2, model), BF16),
            vmem((4, model), BF16),
            vmem((8, model), F32),
            vmem(segs.shape, jnp.int32),
            vmem(short_taps.shape, F32),
            vmem((n_fsdp, 6 * (short_taps.shape[2] // LANES), LANES), F32),
            vmem((n_fsdp, 4 * (short_taps.shape[2] // LANES), LANES), F32),
            vmem(rates.shape, F32),
            vmem(rates.shape, F32),
            vmem(skip.shape, F32),
            vmem((8 + per, LANES), F32),
            vmem((members, rows, width), BF16),
            vmem((members, rows, width), BF16),
            vmem((rows, model), BF16),
            vmem((members, rows, width), BF16),
            vmem((members, rows, width), BF16),
            vmem((blocks, lane_tiles, *square), F32),
            vmem((blocks, lane_tiles, *square), F32),
            vmem((lane_tiles, BLOCK, PACK * BLOCK), BF16),
            vmem((lane_tiles, BLOCK, 2 * BLOCK), BF16),
            vmem((lane_tiles, BLOCK, 3 * BLOCK), BF16),
            vmem((lane_tiles, *square), F32),
            vmem((lane_tiles, *square), F32),
            vmem((MODES, width), BF16),
            vmem((look, MODES, width), BF16),
            dma((6,)),
            dma((n_fsdp,)),
            dma((n_fsdp,)),
            dma((n_fsdp,)),
            dma((n_fsdp,)),
            dma((2,)),
            dma((2,)),
            dma((members,)),
            dma((members,)),
            dma((look,)),
            dma((look,)),
            dma((members,)),
            dma((members,)),
            pltpu.SemaphoreType.REGULAR,
            pltpu.SemaphoreType.REGULAR((max(look - 1, 1),)),
        ],
        compiler_params=pltpu.CompilerParams(
            collective_id=0, has_side_effects=True, vmem_limit_bytes=60 * 1024 * 1024
        ),
    )(streams, segs, short_taps, rates, gains, skip)


def solution(mesh):
    placed = (
        P(None, ("ctx", "fsdp"), None),
        P(),
        P(None, None, "fsdp"),
        P("fsdp", None),
        P("fsdp", None),
        P("fsdp"),
    )
    return jax.shard_map(
        local, mesh=mesh, in_specs=placed, out_specs=P(("ctx", "fsdp"), None), check_vma=False
    )
```
